512 devices in a mesh: led: 32 (over z, core), tile: 16 (over y, x).
Axes of the slice: x: 4, y: 4, z: 16, core: 2. Of those that a mesh axis runs over, the one named last changes fastest.
Arguments:
- spectrum: float32 [16, 8, 16, 32, 4096], P(None, None, 'tile', 'led'), may hold values from -6 to 6
- intensities: bfloat16 [32, 1024, 1024], P('led', 'tile'), may hold values from 0 to 2
- led_of_slot: int32 [32], replicated, may hold values from 0 to 31, each once
- row_offset: int32 [32], replicated, may hold values from 0 to 120
- col_offset: int32 [32], replicated, may hold values from 0 to 56
- tile_mask: int32 [32, 8, 8], replicated, may hold values 0 or 1
- aberration: float32 [5], replicated, may hold values from -1.5 to 1.5
Outputs:
- updated: float32 [16, 8, 16, 32, 4096], P(None, None, 'tile', 'led')
The draws below stay inside these ranges and needn't reach their ends.
Inputs may be any that keep to these rules, and one draw needn't show every extreme that they name: `led_of_slot`: every LED is imaged in exactly one slot.
All inputs are finite; a program needn't handle non-finite values.
Results may differ from the reference program's by a relative error of at most 0.0003.
Values sent between devices are 32-bit elements; how exact they have to be, the bound alone decides.
A program may use at most 64 MiB of HBM per device.

```python
import jax
import jax.numpy as jnp
from jax import lax

M = 1024
TILE = 128
GR = 16
GC = 8
L_DEV = 1
TW = 8
BAND = 64
CU = 32
LEDS = 32
N_LED = 32
N_TILE = 16


def with_ends(result, rng, least, top_value):
    longest = result.shape.index(max(result.shape))
    spots = []
    for shift in (0, 1):
        where = [jax.random.randint(jax.random.fold_in(rng, axis), (), 0, length) for axis, length in enumerate(result.shape)]
        where[longest] = (where[longest] + shift) % result.shape[longest]
        spots.append(tuple(where))
    return result.at[spots[0]].set(least).at[spots[1]].set(top_value)


def block_levels(key, shape, split, least, top_value):
    gain, own = 1.0, jax.random.fold_in(key, 6)
    for dim, blocks in split:
        steps = jnp.exp(jax.random.uniform(jax.random.fold_in(own, dim), (blocks,), jnp.float32, least / len(split), top_value / len(split)))
        gain = gain * jnp.repeat(steps, shape[dim] // blocks).reshape([-1 if axis == dim else 1 for axis in range(len(shape))])
    return gain


def bell_draw(key, dims, scale, limit, cuts=(), kind=jnp.bfloat16):
    entries = jax.random.normal(key, dims, jnp.float32) * scale
    if len(cuts) > 0:
        entries = block_levels(key, dims, cuts, -0.22, 0.18) * entries
    return jnp.clip(entries, min=-limit, max=limit).astype(kind)


def setup_inputs(seed: int = 0) -> dict:
    keys = jax.random.split(jax.random.key(seed), 8)
    return {
        "spectrum": bell_draw(keys[0], (GR, GC, N_TILE, N_LED, 2 * BAND * CU), 1.0, 6.0, ((2, 16), (3, 32)), jnp.float32),
        "intensities": jnp.clip(2.0 * jax.random.uniform(keys[1], (LEDS, M, M), jnp.float32) ** block_levels(keys[1], (LEDS, M, M), ((0, 32), (1, 16)), -0.2, 0.2), 0.0, 2.0).astype(jnp.bfloat16),
        "led_of_slot": jax.random.permutation(keys[2], LEDS).astype(jnp.int32),
        "row_offset": with_ends(jax.random.randint(keys[3], (LEDS,), 0, GR * TW - TW + 1), jax.random.fold_in(keys[3], 1), 0, GR * TW - TW).astype(jnp.int32),
        "col_offset": with_ends(jax.random.randint(keys[4], (LEDS,), 0, GC * TW - TW + 1), jax.random.fold_in(keys[4], 1), 0, GC * TW - TW).astype(jnp.int32),
        "tile_mask": with_ends((jax.random.randint(keys[5], (LEDS, TW, TW), 0, 4) < 3).astype(jnp.int32), jax.random.fold_in(keys[5], 1), 0, 1),
        "aberration": jnp.clip(jax.random.uniform(keys[6], (5,), jnp.float32, -1.5, 1.5), -1.5, 1.5),
    }


STEP_SIZE = 0.25


def aberration_phase(aberration, coord_p, coord_q):
    radial = coord_p * coord_p + coord_q * coord_q
    return (aberration[0] * (2.0 * radial - 1.0)
            + aberration[1] * (coord_p * coord_p - coord_q * coord_q)
            + aberration[2] * (2.0 * coord_p * coord_q)
            + aberration[3] * ((3.0 * radial - 2.0) * coord_p)
            + aberration[4] * ((3.0 * radial - 2.0) * coord_q))


def reference(spectrum, intensities, led_of_slot, row_offset, col_offset, tile_mask, aberration):
    band_rows = M // N_TILE
    unit_cols = M // N_LED
    pieces = spectrum.reshape(GR, GC, N_TILE, N_LED, 2, band_rows, unit_cols)
    whole_field = jnp.transpose(pieces, (4, 0, 2, 5, 1, 3, 6)).reshape(2, GR * M, GC * M)
    halfway = M // 2
    coords = (jnp.arange(M, dtype=jnp.int32) - halfway).astype(jnp.float32) / halfway
    phase_map = aberration_phase(aberration, coords[:, None], coords[None, :])
    phase_cos = jnp.cos(phase_map)
    phase_sin = jnp.sin(phase_map)
    blocks = jnp.arange(M, dtype=jnp.int32) // TILE

    def one_slot(grad_sum, slot_index):
        led_index = led_of_slot[slot_index]
        row_start = (row_offset[led_index] * TILE).astype(jnp.int32)
        col_start = (col_offset[led_index] * TILE).astype(jnp.int32)
        anchor = jnp.zeros((), jnp.int32)
        window = lax.dynamic_slice(whole_field, (anchor, row_start, col_start), (2, M, M))
        gate_map = tile_mask[led_index].astype(jnp.float32)[blocks][:, blocks]
        pupil_map = gate_map * (phase_cos + 1j * phase_sin)
        masked_field = pupil_map * (window[0] + 1j * window[1])
        wave_field = jnp.fft.ifft2(masked_field) * M
        measured = intensities[slot_index].astype(jnp.float32).T
        excess = jnp.real(wave_field) ** 2 + jnp.imag(wave_field) ** 2 - measured
        back_field = jnp.fft.fft2(excess * wave_field) / M
        grad_piece = jnp.conj(pupil_map) * back_field
        current = lax.dynamic_slice(grad_sum, (anchor, row_start, col_start), (2, M, M))
        current = current + jnp.stack([jnp.real(grad_piece), jnp.imag(grad_piece)]).astype(grad_sum.dtype)
        return lax.dynamic_update_slice(grad_sum, current, (anchor, row_start, col_start)), None

    grad_sum, _ = lax.scan(one_slot, jnp.zeros_like(whole_field), jnp.arange(L_DEV * N_LED, dtype=jnp.int32))
    updated = whole_field - STEP_SIZE * grad_sum
    updated = updated.reshape(2, GR, N_TILE, band_rows, GC, N_LED, unit_cols)
    return jnp.transpose(updated, (1, 4, 2, 5, 0, 3, 6)).reshape(spectrum.shape)
```

```python
import math

import jax
import jax.numpy as jnp
import numpy as np
from jax import lax
from jax.experimental import pallas as pl
from jax.experimental.pallas import tpu as pltpu
from jax.sharding import PartitionSpec as P

M = 1024
TILE = 128
GR = 16
GC = 8
N_LED = 32
N_TILE = 16
BAND = M // N_TILE
CU = M // N_LED
LINES = BAND * CU // 128
STEP_SIZE = 0.25
MESH = pl.DeviceIdType.MESH


def turn(re, im, angle):
    eighth = round(angle / (math.pi / 4.0), 9)
    if eighth == int(eighth) and int(eighth) % 2 == 0:
        quarter = int(eighth) // 2 % 4
        return ((re, im), (-im, re), (-re, -im), (im, -re))[quarter]
    cos, sin = math.cos(angle), math.sin(angle)
    return re * cos - im * sin, im * cos + re * sin


def fft_points(parts, sign):
    count = len(parts)
    if count == 1:
        return list(parts)
    if count == 2:
        (ar, ai), (br, bi) = parts
        return [(ar + br, ai + bi), (ar - br, ai - bi)]
    quarter = count // 4
    subs = [fft_points(parts[r::4], sign) for r in range(4)]
    out = [None] * count
    for k in range(quarter):
        (ar, ai), (br, bi), (cr, ci), (dr, di) = (
            turn(*subs[r][k], sign * 2.0 * math.pi * r * k / count) for r in range(4)
        )
        sr, si, tr, ti = ar + cr, ai + ci, ar - cr, ai - ci
        ur, ui, vr, vi = br + dr, bi + di, br - dr, bi - di
        out[k] = (sr + ur, si + ui)
        out[k + 2 * quarter] = (sr - ur, si - ui)
        if sign > 0:
            out[k + quarter] = (tr - vi, ti + vr)
            out[k + 3 * quarter] = (tr + vi, ti - vr)
        else:
            out[k + quarter] = (tr + vi, ti - vr)
            out[k + 3 * quarter] = (tr - vi, ti + vr)
    return out


def digit(shape, axis, unit):
    return lax.broadcasted_iota(jnp.int32, shape, axis) // unit


def swapped(x, distance, axis):
    size = x.shape[axis]
    if 2 * distance == size:
        return pltpu.roll(x, distance, axis)
    low = digit(x.shape, axis, distance) % 2 == 0
    return jnp.where(low, pltpu.roll(x, size - distance, axis), pltpu.roll(x, distance, axis))


def four_forward(re, im, axis, unit):
    group = digit(re.shape, axis, unit)
    first = jnp.where(group < 2, 1.0, -1.0)
    second = jnp.where(group % 2 == 0, 1.0, -1.0)
    re = first * re + swapped(re, 2 * unit, axis)
    im = first * im + swapped(im, 2 * unit, axis)
    re, im = jnp.where(group == 3, -im, re), jnp.where(group == 3, re, im)
    return second * re + swapped(re, unit, axis), second * im + swapped(im, unit, axis)


def four_backward(re, im, axis, unit):
    group = digit(re.shape, axis, unit)
    first = jnp.where(group < 2, 1.0, -1.0)
    second = jnp.where(group % 2 == 0, 1.0, -1.0)
    re, im = second * re + swapped(re, unit, axis), second * im + swapped(im, unit, axis)
    re, im = jnp.where(group == 3, im, re), jnp.where(group == 3, -re, im)
    return first * re + swapped(re, 2 * unit, axis), first * im + swapped(im, 2 * unit, axis)


def cos_sin(phase):
    count = jnp.floor(phase * (2.0 / math.pi) + 0.5)
    rest = phase - count * 1.5703125
    rest = rest - count * 4.837512969970703125e-4
    rest = rest - count * 7.54978995489188216e-8
    square = rest * rest
    sin_rest = ((-1.9515295891e-4 * square + 8.3321608736e-3) * square - 1.6666654611e-1) * square * rest + rest
    cos_rest = (
        (2.443315711809948e-5 * square - 1.388731625493765e-3) * square + 4.166664568298827e-2
    ) * square * square - 0.5 * square + 1.0
    quadrant = count.astype(jnp.int32) & 3
    odd = (quadrant & 1) == 1
    cos = jnp.where(odd, sin_rest, cos_rest)
    sin = jnp.where(odd, cos_rest, sin_rest)
    cos = jnp.where((quadrant == 1) | (quadrant == 2), -cos, cos)
    return cos, jnp.where(quadrant >= 2, -sin, sin)


def halves(x):
    high = x.astype(jnp.bfloat16)
    return high, (x - high.astype(jnp.float32)).astype(jnp.bfloat16)


def product(left, right, dims):
    def one(a, b):
        return lax.dot_general(a, b, (dims, ((), ())), preferred_element_type=jnp.float32)

    return one(left[0], right[0]) + (one(left[0], right[1]) + one(left[1], right[0]))


def window_row(led_ref, row_ref, col_ref, slot, tile_here, led_here):
    led = led_ref[slot]
    row_start = row_ref[led] * TILE
    col_start = col_ref[led] * TILE
    row_group = (row_start + ((tile_here * BAND - row_start) & (M - 1))) >> 10
    col_group = (col_start + ((led_here * CU - col_start) & (M - 1))) >> 10
    return row_group * GC + col_group


def exchange_kernel(
    led_ref, row_ref, col_ref, mask_ref, aber_ref, spec_ref, image_ref, table_hi_ref, table_lo_ref,
    turn_u_ref, turn_j_ref, turn_h_ref, out_ref,
    outgoing, window, pupil, lines, lines_hi, lines_lo, bands_out, bands_in, cells, back_out, back_in,
    grad_out, grad_in, led_send, led_recv, tile_send, tile_recv, back_send, back_recv, grad_send, grad_recv,
):
    led_here = lax.axis_index("led")
    tile_here = lax.axis_index("tile")

    barrier = pltpu.get_barrier_semaphore()

    @pl.loop(1, N_LED)
    def _(step):
        pl.semaphore_signal(barrier, inc=1, device_id={"led": (led_here + step) % N_LED}, device_id_type=MESH)

    @pl.loop(1, N_TILE)
    def _(step):
        pl.semaphore_signal(barrier, inc=1, device_id={"tile": (tile_here + step) % N_TILE}, device_id_type=MESH)

    @pl.loop(0, N_LED)
    def _(slot):
        outgoing[slot] = spec_ref[window_row(led_ref, row_ref, col_ref, slot, tile_here, led_here)]

    def led_copy(src, dst, sends, recvs, peer):
        return pltpu.make_async_remote_copy(
            src_ref=src.at[peer], dst_ref=dst.at[led_here], send_sem=sends.at[peer], recv_sem=recvs.at[led_here],
            device_id={"led": peer}, device_id_type=MESH,
        )

    def led_arrival(src, dst, sends, recvs, peer):
        return pltpu.make_async_remote_copy(
            src_ref=src.at[peer], dst_ref=dst.at[peer], send_sem=sends.at[peer], recv_sem=recvs.at[peer],
            device_id={"led": peer}, device_id_type=MESH,
        )

    def tile_copy(src, dst, sends, recvs, peer):
        return pltpu.make_async_remote_copy(
            src_ref=src.at[peer], dst_ref=dst.at[tile_here], send_sem=sends.at[peer], recv_sem=recvs.at[tile_here],
            device_id={"tile": peer}, device_id_type=MESH,
        )

    def tile_arrival(src, dst, sends, recvs, peer):
        return pltpu.make_async_remote_copy(
            src_ref=src.at[peer], dst_ref=dst.at[peer], send_sem=sends.at[peer], recv_sem=recvs.at[peer],
            device_id={"tile": peer}, device_id_type=MESH,
        )

    def send_all(copy, count, here, *refs):
        @pl.loop(1, count)
        def _(step):
            ahead = (step + 1) // 2
            shift = jnp.where(step % 2 == 1, ahead, count - ahead)
            copy(*refs, (here + shift) % count).start()

    def wait_arrivals(arrival, count, here, *refs):
        @pl.loop(1, count)
        def _(step):
            arrival(*refs, (here + step) % count).wait_recv()

    def wait_sends(arrival, count, here, *refs):
        @pl.loop(1, count)
        def _(step):
            arrival(*refs, (here + step) % count).wait_send()

    pl.semaphore_wait(barrier, N_LED + N_TILE - 2)

    led_refs = (outgoing, window, led_send, led_recv)
    send_all(led_copy, N_LED, led_here, *led_refs)
    window[led_here] = outgoing[led_here]

    led = led_ref[led_here]
    row_start = row_ref[led] * TILE
    col_start = col_ref[led] * TILE
    lane = lax.broadcasted_iota(jnp.int32, (16, 128), 1)
    sub = lax.broadcasted_iota(jnp.int32, (16, 128), 0)
    row_first = (tile_here * BAND - row_start) & (M - 1)
    row_window = row_first + 4 * sub + lane // CU
    coord_p = (row_window - M // 2).astype(jnp.float32) * (1.0 / (M // 2))

    @pl.loop(0, N_LED)
    def _(part):
        col_first = (part * CU - col_start) & (M - 1)
        coord_q = (col_first + lane % CU - M // 2).astype(jnp.float32) * (1.0 / (M // 2))
        radial = coord_p * coord_p + coord_q * coord_q
        phase = (
            aber_ref[0] * (2.0 * radial - 1.0)
            + aber_ref[1] * (coord_p * coord_p - coord_q * coord_q)
            + aber_ref[2] * (2.0 * coord_p * coord_q)
            + aber_ref[3] * ((3.0 * radial - 2.0) * coord_p)
            + aber_ref[4] * ((3.0 * radial - 2.0) * coord_q)
        )
        gate = mask_ref[led * 64 + (row_first >> 7) * 8 + (col_first >> 7)].astype(jnp.float32)
        cos, sin = cos_sin(phase)
        pupil[0, part] = gate * cos
        pupil[1, part] = gate * sin

    wait_arrivals(led_arrival, N_LED, led_here, *led_refs)

    table = (table_hi_ref[...], table_lo_ref[...])

    @pl.loop(0, 2)
    def _(half):
        start = pl.multiple_of(half * 8, 8)
        parts = []
        for part in range(N_LED):
            pr, pi = pupil[0, part, pl.ds(start, 8)], pupil[1, part, pl.ds(start, 8)]
            wr, wi = window[part, pl.ds(start, 8)], window[part, pl.ds(16 + start, 8)]
            parts.append((pr * wr - pi * wi, pr * wi + pi * wr))
        for low, (re, im) in enumerate(fft_points(parts, 1.0)):
            cos, sin = turn_u_ref[0, pl.ds(low, 1)], turn_u_ref[1, pl.ds(low, 1)]
            lines[0, pl.ds(low * 16 + start, 8)] = re * cos - im * sin
            lines[1, pl.ds(low * 16 + start, 8)] = im * cos + re * sin

    @pl.loop(0, 16)
    def _(line):
        start = pl.multiple_of(line * 32, 32)
        for c in range(2):
            high, low = halves(lines[c, pl.ds(line, 32, stride=16)])
            lines_hi[pl.ds(start, 32), c * 128 : c * 128 + 128] = high
            lines_lo[pl.ds(start, 32), c * 128 : c * 128 + 128] = low

    bands_out[...] = product(table, (lines_hi[...], lines_lo[...]), ((1,), (1,))).reshape(16, 2, 8, 512)

    tile_refs = (bands_out, bands_in, tile_send, tile_recv)
    send_all(tile_copy, N_TILE, tile_here, *tile_refs)
    bands_in[tile_here] = bands_out[tile_here]
    wait_arrivals(tile_arrival, N_TILE, tile_here, *tile_refs)

    points = fft_points([(bands_in[k, 0], bands_in[k, 1]) for k in range(16)], 1.0)
    for low in range(16):
        re, im = points[low]
        quads = [
            turn(re[:, q * 128 : q * 128 + 128], im[:, q * 128 : q * 128 + 128], 2.0 * math.pi * low * q / 64)
            for q in range(4)
        ]
        for high, (qr, qi) in enumerate(fft_points(quads, 1.0)):
            cells[0, low + 16 * high] = qr
            cells[1, low + 16 * high] = qi

    @pl.loop(0, 8)
    def _(chunk):
        span = pl.ds(pl.multiple_of(chunk * 8, 8), 8)
        jr, ji = turn_j_ref[0, span], turn_j_ref[1, span]
        hr, hi = turn_h_ref[0][None], turn_h_ref[1][None]
        re, im = cells[0, span], cells[1, span]
        re, im = re * jr - im * ji, im * jr + re * ji
        re, im = four_forward(re, im, 2, 32)
        re, im = re * hr - im * hi, im * hr + re * hi
        re, im = four_forward(re, im, 1, 2)
        excess = re * re + im * im - image_ref[span]
        re, im = excess * re, excess * im
        re, im = four_backward(re, im, 1, 2)
        re, im = re * hr + im * hi, im * hr - re * hi
        re, im = four_backward(re, im, 2, 32)
        cells[0, span] = re * jr + im * ji
        cells[1, span] = im * jr - re * ji

    points = []
    for low in range(16):
        quads = fft_points([(cells[0, low + 16 * q], cells[1, low + 16 * q]) for q in range(4)], -1.0)
        quads = [turn(*quads[q], -2.0 * math.pi * low * q / 64) for q in range(4)]
        points.append(tuple(jnp.concatenate([quads[q][c] for q in range(4)], axis=1) for c in range(2)))
    for k, (re, im) in enumerate(fft_points(points, -1.0)):
        back_out[k, 0] = re
        back_out[k, 1] = im

    back_refs = (back_out, back_in, back_send, back_recv)
    send_all(tile_copy, N_TILE, tile_here, *back_refs)
    back_in[tile_here] = back_out[tile_here]
    wait_arrivals(tile_arrival, N_TILE, tile_here, *back_refs)

    mixed = product(halves(back_in[...].reshape(256, 512)), table, ((0,), (0,)))
    lines[0] = mixed[:, 0:128]
    lines[1] = mixed[:, 128:256]

    @pl.loop(0, 2)
    def _(half):
        start = pl.multiple_of(half * 8, 8)
        parts = []
        for low in range(N_LED):
            re, im = (lines[c, pl.ds(half * 256 + low, 8, stride=32)] for c in range(2))
            cos, sin = turn_u_ref[0, pl.ds(low, 1)], turn_u_ref[1, pl.ds(low, 1)]
            parts.append((re * cos + im * sin, im * cos - re * sin))
        for part, (re, im) in enumerate(fft_points(parts, -1.0)):
            pr, pi = pupil[0, part, pl.ds(start, 8)], pupil[1, part, pl.ds(start, 8)]
            grad_out[part, pl.ds(start, 8)] = pr * re + pi * im
            grad_out[part, pl.ds(16 + start, 8)] = pr * im - pi * re

    grad_refs = (grad_out, grad_in, grad_send, grad_recv)
    send_all(led_copy, N_LED, led_here, *grad_refs)
    grad_in[led_here] = grad_out[led_here]
    wait_arrivals(led_arrival, N_LED, led_here, *grad_refs)
    out_ref[...] = grad_in[...]

    wait_sends(led_arrival, N_LED, led_here, *led_refs)
    wait_sends(tile_arrival, N_TILE, tile_here, *tile_refs)
    wait_sends(tile_arrival, N_TILE, tile_here, *back_refs)
    wait_sends(led_arrival, N_LED, led_here, *grad_refs)


def update_kernel(led_ref, row_ref, col_ref, spec_ref, grad_ref, out_ref):
    led_here = lax.axis_index("led")
    tile_here = lax.axis_index("tile")
    out_ref[...] = spec_ref[...]

    @pl.loop(0, N_LED)
    def _(slot):
        row = window_row(led_ref, row_ref, col_ref, slot, tile_here, led_here)
        out_ref[row] = out_ref[row] - STEP_SIZE * grad_ref[slot]


def dft_tables():
    rank = np.arange(256)
    out_re = (rank // 8) % 2
    out_b = 2 * (rank // 16) + rank % 2
    out_j = (rank // 2) % 4
    in_re = rank // 128
    in_j = (rank // 32) % 4
    in_u = rank % 32
    angle = 2.0 * np.pi * ((out_b[:, None] * in_u[None, :]) % 32) / 32.0
    same = out_j[:, None] == in_j[None, :]
    real = np.where(
        out_re[:, None] == in_re[None, :], np.cos(angle), np.where(out_re[:, None] == 0, -np.sin(angle), np.sin(angle))
    )
    table = (same * real / M).astype(np.float32)
    table_hi = table.astype(jnp.bfloat16)
    table_lo = (table - table_hi.astype(np.float32)).astype(jnp.bfloat16)
    lane = np.arange(128)

    def turns(product, modulus):
        angle = 2.0 * np.pi * (product % modulus) / modulus
        return np.stack([np.cos(angle), np.sin(angle)]).astype(np.float32)

    turn_u = turns(np.arange(32)[:, None] * (lane % 32)[None, :], M)
    sub_j = np.arange(8) // 2
    turn_j = turns(np.arange(64)[:, None, None] * (4 * (lane // 32)[None, None, :] + sub_j[None, :, None]), M)
    frequency = np.array([0, 2, 1, 3])
    turn_h = turns(sub_j[:, None] * frequency[lane // 32][None, :], 16)
    return table_hi, table_lo, turn_u, turn_j, turn_h


def arrange_image(image):
    order = np.array([0, 2, 1, 3])
    cut = image.reshape(2, 32, 4, 4, 64)[:, :, order][:, :, :, order]
    return jnp.transpose(cut, (4, 2, 0, 3, 1)).reshape(64, 8, 128)


def shards(spectrum, intensities, led_of_slot, row_offset, col_offset, tile_mask, aberration):
    rows = spectrum.reshape(GR * GC, LINES * 2, 128)
    image = arrange_image(intensities.reshape(BAND, M)).astype(jnp.float32)
    table_hi, table_lo, turn_u, turn_j, turn_h = (jnp.asarray(t) for t in dft_tables())
    smem = pl.BlockSpec(memory_space=pltpu.SMEM)
    vmem = pl.BlockSpec(memory_space=pltpu.VMEM)
    message = pltpu.VMEM((N_LED, 32, 128), jnp.float32)
    band = pltpu.VMEM((N_TILE, 2, 8, 512), jnp.float32)
    leds = pltpu.SemaphoreType.DMA((N_LED,))
    tiles = pltpu.SemaphoreType.DMA((N_TILE,))
    grad = pl.pallas_call(
        exchange_kernel,
        out_shape=jax.ShapeDtypeStruct((N_LED, 32, 128), jnp.float32),
        in_specs=[smem] * 5 + [vmem] * 7,
        out_specs=vmem,
        scratch_shapes=[
            message,
            message,
            pltpu.VMEM((2, N_LED, 16, 128), jnp.float32),
            pltpu.VMEM((2, 512, 128), jnp.float32),
            pltpu.VMEM((512, 256), jnp.bfloat16),
            pltpu.VMEM((512, 256), jnp.bfloat16),
            band,
            band,
            pltpu.VMEM((2, 64, 8, 128), jnp.float32),
            band,
            band,
            message,
            message,
            leds,
            leds,
            tiles,
            tiles,
            tiles,
            tiles,
            leds,
            leds,
        ],
        compiler_params=pltpu.CompilerParams(
            collective_id=0, has_side_effects=True, vmem_limit_bytes=40 * 1024 * 1024
        ),
    )(
        led_of_slot, row_offset, col_offset, tile_mask.reshape(-1), aberration, rows, image,
        table_hi, table_lo, turn_u, turn_j, turn_h,
    )
    updated = pl.pallas_call(
        update_kernel,
        out_shape=jax.ShapeDtypeStruct((GR * GC, LINES * 2, 128), jnp.float32),
        in_specs=[smem] * 3 + [vmem] * 2,
        out_specs=vmem,
        compiler_params=pltpu.CompilerParams(vmem_limit_bytes=24 * 1024 * 1024),
    )(led_of_slot, row_offset, col_offset, rows, grad)
    return updated.reshape(spectrum.shape)


def solution(mesh):
    placed = (P(None, None, "tile", "led", None), P("led", "tile", None), P(), P(), P(), P(), P())
    return jax.shard_map(
        shards,
        mesh=mesh,
        in_specs=placed,
        out_specs=P(None, None, "tile", "led", None),
        check_vma=False,
    )
```

```python
import math

import jax
import jax.numpy as jnp
from jax import lax
from jax.experimental import pallas as pl
from jax.experimental.pallas import tpu as pltpu
from jax.sharding import PartitionSpec as P

M = 1024
TILE = 128
GR = 16
GC = 8
N_LED = 32
N_TILE = 16
BAND = M // N_TILE
CU = M // N_LED
LINES = BAND * CU // 128
STEP_SIZE = 0.25
MESH = pl.DeviceIdType.MESH


def turn(re, im, angle):
    eighth = round(angle / (math.pi / 4.0), 9)
    if eighth == int(eighth) and int(eighth) % 2 == 0:
        quarter = int(eighth) // 2 % 4
        return ((re, im), (-im, re), (-re, -im), (im, -re))[quarter]
    cos, sin = math.cos(angle), math.sin(angle)
    return re * cos - im * sin, im * cos + re * sin


def fft_points(parts, sign):
    count = len(parts)
    if count == 1:
        return list(parts)
    if count == 2:
        (ar, ai), (br, bi) = parts
        return [(ar + br, ai + bi), (ar - br, ai - bi)]
    quarter = count // 4
    subs = [fft_points(parts[r::4], sign) for r in range(4)]
    out = [None] * count
    for k in range(quarter):
        (ar, ai), (br, bi), (cr, ci), (dr, di) = (
            turn(*subs[r][k], sign * 2.0 * math.pi * r * k / count) for r in range(4)
        )
        sr, si, tr, ti = ar + cr, ai + ci, ar - cr, ai - ci
        ur, ui, vr, vi = br + dr, bi + di, br - dr, bi - di
        out[k] = (sr + ur, si + ui)
        out[k + 2 * quarter] = (sr - ur, si - ui)
        if sign > 0:
            out[k + quarter] = (tr - vi, ti + vr)
            out[k + 3 * quarter] = (tr + vi, ti - vr)
        else:
            out[k + quarter] = (tr + vi, ti - vr)
            out[k + 3 * quarter] = (tr - vi, ti + vr)
    return out


def digit(shape, axis, unit):
    return lax.broadcasted_iota(jnp.int32, shape, axis) // unit


def swapped(x, distance, axis):
    size = x.shape[axis]
    if 2 * distance == size:
        return pltpu.roll(x, distance, axis)
    low = digit(x.shape, axis, distance) % 2 == 0
    return jnp.where(low, pltpu.roll(x, size - distance, axis), pltpu.roll(x, distance, axis))


def four_forward(re, im, axis, unit):
    group = digit(re.shape, axis, unit)
    first = jnp.where(group < 2, 1.0, -1.0)
    second = jnp.where(group % 2 == 0, 1.0, -1.0)
    re = first * re + swapped(re, 2 * unit, axis)
    im = first * im + swapped(im, 2 * unit, axis)
    re, im = jnp.where(group == 3, -im, re), jnp.where(group == 3, re, im)
    return second * re + swapped(re, unit, axis), second * im + swapped(im, unit, axis)


def four_backward(re, im, axis, unit):
    group = digit(re.shape, axis, unit)
    first = jnp.where(group < 2, 1.0, -1.0)
    second = jnp.where(group % 2 == 0, 1.0, -1.0)
    re, im = second * re + swapped(re, unit, axis), second * im + swapped(im, unit, axis)
    re, im = jnp.where(group == 3, im, re), jnp.where(group == 3, -re, im)
    return first * re + swapped(re, 2 * unit, axis), first * im + swapped(im, 2 * unit, axis)


def cos_sin(phase):
    count = jnp.floor(phase * (2.0 / math.pi) + 0.5)
    rest = phase - count * 1.5703125
    rest = rest - count * 4.837512969970703125e-4
    rest = rest - count * 7.54978995489188216e-8
    square = rest * rest
    sin_rest = ((-1.9515295891e-4 * square + 8.3321608736e-3) * square - 1.6666654611e-1) * square * rest + rest
    cos_rest = (
        (2.443315711809948e-5 * square - 1.388731625493765e-3) * square + 4.166664568298827e-2
    ) * square * square - 0.5 * square + 1.0
    quadrant = count.astype(jnp.int32) & 3
    odd = (quadrant & 1) == 1
    cos = jnp.where(odd, sin_rest, cos_rest)
    sin = jnp.where(odd, cos_rest, sin_rest)
    cos = jnp.where((quadrant == 1) | (quadrant == 2), -cos, cos)
    return cos, jnp.where(quadrant >= 2, -sin, sin)


def halves(x):
    high = x.astype(jnp.bfloat16)
    return high, (x - high.astype(jnp.float32)).astype(jnp.bfloat16)


def product(left, right, dims):
    def one(a, b):
        return lax.dot_general(a, b, (dims, ((), ())), preferred_element_type=jnp.float32)

    return one(left[0], right[0]) + (one(left[0], right[1]) + one(left[1], right[0]))


def window_row(led_ref, row_ref, col_ref, slot, tile_here, led_here):
    led = led_ref[slot]
    row_start = row_ref[led] * TILE
    col_start = col_ref[led] * TILE
    row_group = (row_start + ((tile_here * BAND - row_start) & (M - 1))) >> 10
    col_group = (col_start + ((led_here * CU - col_start) & (M - 1))) >> 10
    return row_group * GC + col_group


def exchange_kernel(
    led_ref, row_ref, col_ref, mask_ref, aber_ref, spec_hbm, image_hbm, out_ref,
    spec, measured, image, table_hi, table_lo, turn_u, turn_j,
    outgoing, window, pupil, lines, lines_hi, lines_lo, bands_out, bands_in, cells, back_out, back_in,
    grad_out, grad_in, spec_sem, image_sem,
    led_send, led_recv, tile_send, tile_recv, back_send, back_recv, grad_send, grad_recv,
):
    led_here = lax.axis_index("led")
    tile_here = lax.axis_index("tile")

    spec_copy = pltpu.make_async_copy(spec_hbm, spec, spec_sem)
    image_copy = pltpu.make_async_copy(image_hbm, measured, image_sem)
    spec_copy.start()
    image_copy.start()
    barrier = pltpu.get_barrier_semaphore()

    def far_first(step, count, here):
        away = step // 2
        return (here + count // 2 + jnp.where(step % 2 == 1, away, -away)) % count

    @pl.loop(1, N_LED)
    def _(step):
        peer = far_first(step, N_LED, led_here)
        pl.semaphore_signal(barrier, inc=1, device_id={"led": peer}, device_id_type=MESH)

    @pl.loop(1, N_TILE)
    def _(step):
        peer = far_first(step, N_TILE, tile_here)
        pl.semaphore_signal(barrier, inc=1, device_id={"tile": peer}, device_id_type=MESH)

    def led_copy(src, dst, sends, recvs, half, peer, origin):
        return pltpu.make_async_remote_copy(
            src_ref=src.at[half, peer], dst_ref=dst.at[half, origin],
            send_sem=sends.at[half, peer], recv_sem=recvs.at[half, origin],
            device_id={"led": peer}, device_id_type=MESH,
        )

    def tile_copy(src, dst, sends, recvs, half, peer, origin):
        return pltpu.make_async_remote_copy(
            src_ref=src.at[half, peer], dst_ref=dst.at[half, origin],
            send_sem=sends.at[half, peer], recv_sem=recvs.at[half, origin],
            device_id={"tile": peer}, device_id_type=MESH,
        )

    led_axis = (led_copy, N_LED, led_here)
    tile_axis = (tile_copy, N_TILE, tile_here)

    def send_half(axis, half, src, dst, sends, recvs):
        copy, count, here = axis

        @pl.loop(1, count)
        def _(step):
            copy(src, dst, sends, recvs, half, far_first(step, count, here), here).start()

        dst[half, here] = src[half, here]

    def wait_half(axis, half, src, dst, sends, recvs):
        copy, count, here = axis

        @pl.loop(1, count)
        def _(step):
            peer = far_first(step, count, here)
            copy(src, dst, sends, recvs, half, peer, peer).wait_recv()

    def wait_sent(axis, src, dst, sends, recvs):
        copy, count, here = axis

        @pl.loop(1, count)
        def _(step):
            peer = far_first(step, count, here)
            copy(src, dst, sends, recvs, 0, peer, peer).wait_send()
            copy(src, dst, sends, recvs, 1, peer, peer).wait_send()

    spec_copy.wait()

    @pl.loop(0, N_LED)
    def _(slot):
        row = window_row(led_ref, row_ref, col_ref, slot, tile_here, led_here)
        for half in range(2):
            for c in range(2):
                outgoing[half, slot, c] = spec[row, c * 16 + half * 8 : c * 16 + half * 8 + 8]

    def turns(index, modulus):
        return cos_sin((index & (modulus - 1)).astype(jnp.float32) * (2.0 * math.pi / modulus))

    def iota(shape, axis):
        return lax.broadcasted_iota(jnp.int32, shape, axis)

    @pl.loop(0, 8)
    def _(chunk):
        start = pl.multiple_of(chunk * 32, 32)
        rank = start + iota((32, 256), 0)
        entry = iota((32, 256), 1)
        cos, sin = turns((2 * (rank >> 4) + (rank & 1)) * (entry & 31), 32)
        out_im, in_im = (rank >> 3) & 1, entry >> 7
        value = jnp.where(out_im == in_im, cos, jnp.where(out_im == 0, -sin, sin))
        value = jnp.where(((rank >> 1) & 3) == ((entry >> 5) & 3), value * (1.0 / M), 0.0)
        high, low = halves(value)
        table_hi[pl.ds(start, 32), :] = high
        table_lo[pl.ds(start, 32), :] = low

    lane8 = iota((8, 128), 1)
    sub8 = iota((8, 128), 0)
    turn_u[0], turn_u[1] = turns(iota((32, 128), 0) * (iota((32, 128), 1) & 31), M)

    @pl.loop(0, 64)
    def _(low):
        turn_j[0, low], turn_j[1, low] = turns(low * (4 * (lane8 >> 5) + (sub8 >> 1)), M)

    chunk8 = lane8 >> 5
    frequency8 = jnp.where(chunk8 == 1, 2, jnp.where(chunk8 == 2, 1, chunk8))
    turn_hr, turn_hi = turns((sub8 >> 1) * frequency8, 16)

    led = led_ref[led_here]
    row_start = row_ref[led] * TILE
    col_start = col_ref[led] * TILE
    lane = iota((16, 128), 1)
    row_first = (tile_here * BAND - row_start) & (M - 1)
    row_window = row_first + 4 * iota((16, 128), 0) + (lane >> 5)
    coord_p = (row_window - M // 2).astype(jnp.float32) * (1.0 / (M // 2))

    @pl.loop(0, N_LED)
    def _(part):
        col_first = (part * CU - col_start) & (M - 1)
        coord_q = (col_first + (lane & 31) - M // 2).astype(jnp.float32) * (1.0 / (M // 2))
        radial = coord_p * coord_p + coord_q * coord_q
        phase = (
            aber_ref[0] * (2.0 * radial - 1.0)
            + aber_ref[1] * (coord_p * coord_p - coord_q * coord_q)
            + aber_ref[2] * (2.0 * coord_p * coord_q)
            + aber_ref[3] * ((3.0 * radial - 2.0) * coord_p)
            + aber_ref[4] * ((3.0 * radial - 2.0) * coord_q)
        )
        gate = mask_ref[(row_first >> 7) * 8 + (col_first >> 7), led].astype(jnp.float32)
        cos, sin = cos_sin(phase)
        pupil[0, part] = gate * cos
        pupil[1, part] = gate * sin

    pl.semaphore_wait(barrier, N_LED + N_TILE - 2)

    led_refs = (outgoing, window, led_send, led_recv)
    send_half(led_axis, 0, *led_refs)
    send_half(led_axis, 1, *led_refs)

    image_copy.wait()
    chunk64 = iota((64, 128), 1) >> 5
    for h in range(4):
        pieces = []
        for block in (2 * h, 2 * h + 1):
            lines_here = measured[0, :, block * 128 : block * 128 + 128].astype(jnp.float32)
            turned = jnp.transpose(jnp.concatenate([lines_here, lines_here], axis=0))
            rolled = pltpu.roll(turned, 32, 1)
            pieces += [(turned[f : f + 64], rolled[f : f + 64]) for f in (0, 64)]
        for s in range(2):
            merged = pieces[0][s]
            for m, f in ((1, 2), (2, 1), (3, 3)):
                merged = jnp.where(chunk64 == m, pieces[f][(m + s) % 2], merged)
            image[pl.ds((0, 2, 1, 3)[h] * 2 + s, 64, stride=8), :] = merged

    tile_refs = (bands_out, bands_in, tile_send, tile_recv)
    table = (table_hi[...], table_lo[...])
    for half in range(2):
        wait_half(led_axis, half, *led_refs)
        parts = []
        for part in range(N_LED):
            pr, pi = (pupil[c, part, half * 8 : half * 8 + 8] for c in range(2))
            wr, wi = window[half, part, 0], window[half, part, 1]
            parts.append((pr * wr - pi * wi, pr * wi + pi * wr))
        for low, (re, im) in enumerate(fft_points(parts, 1.0)):
            cos, sin = turn_u[0, low : low + 1], turn_u[1, low : low + 1]
            lines[0, low * 8 : low * 8 + 8] = re * cos - im * sin
            lines[1, low * 8 : low * 8 + 8] = im * cos + re * sin
        for line in range(8):
            for c in range(2):
                high, low = halves(lines[c, pl.ds(line, 32, stride=8)])
                lines_hi[line * 32 : line * 32 + 32, c * 128 : c * 128 + 128] = high
                lines_lo[line * 32 : line * 32 + 32, c * 128 : c * 128 + 128] = low
        mixed = product(table, (lines_hi[...], lines_lo[...]), ((1,), (1,)))
        bands_out[half] = mixed.reshape(N_TILE, 2, 8, 256)
        send_half(tile_axis, half, *tile_refs)

    for half in range(2):
        wait_half(tile_axis, half, *tile_refs)
        points = fft_points([(bands_in[half, k, 0], bands_in[half, k, 1]) for k in range(N_TILE)], 1.0)
        for low, (re, im) in enumerate(points):
            for side in range(2):
                q = 2 * half + side
                span = slice(side * 128, side * 128 + 128)
                cells[0, q, low], cells[1, q, low] = turn(re[:, span], im[:, span], 2.0 * math.pi * low * q / 64)

    @pl.loop(0, 4)
    def _(chunk):
        span = pl.ds(chunk * 4, 4)
        quads = fft_points([(cells[0, q, span], cells[1, q, span]) for q in range(4)], 1.0)
        back = []
        for q, (re, im) in enumerate(quads):
            where = pl.ds(16 * q + chunk * 4, 4)
            jr, ji = turn_j[0, where], turn_j[1, where]
            hr, hi = turn_hr[None], turn_hi[None]
            re, im = re * jr - im * ji, im * jr + re * ji
            re, im = four_forward(re, im, 2, 32)
            re, im = re * hr - im * hi, im * hr + re * hi
            re, im = four_forward(re, im, 1, 2)
            seen = image[pl.ds(pl.multiple_of((16 * q + chunk * 4) * 8, 32), 32), :].reshape(4, 8, 128)
            excess = re * re + im * im - seen
            re, im = excess * re, excess * im
            re, im = four_backward(re, im, 1, 2)
            re, im = re * hr + im * hi, im * hr - re * hi
            re, im = four_backward(re, im, 2, 32)
            back.append((re * jr + im * ji, im * jr - re * ji))
        for q, (re, im) in enumerate(fft_points(back, -1.0)):
            cells[0, q, span] = re
            cells[1, q, span] = im

    back_refs = (back_out, back_in, back_send, back_recv)
    for half in range(2):
        for side in range(2):
            q = 2 * half + side
            points = [turn(cells[0, q, low], cells[1, q, low], -2.0 * math.pi * low * q / 64) for low in range(16)]
            for k, (re, im) in enumerate(fft_points(points, -1.0)):
                back_out[half, k, 0, :, side * 128 : side * 128 + 128] = re
                back_out[half, k, 1, :, side * 128 : side * 128 + 128] = im
        send_half(tile_axis, half, *back_refs)

    grad_refs = (grad_out, grad_in, grad_send, grad_recv)
    for half in range(2):
        wait_half(tile_axis, half, *back_refs)
        mixed = product(halves(back_in[half].reshape(256, 256)), table, ((0,), (0,)))
        lines[0] = mixed[:, 0:128]
        lines[1] = mixed[:, 128:256]
        parts = []
        for low in range(N_LED):
            re, im = (lines[c, pl.ds(low, 8, stride=32)] for c in range(2))
            cos, sin = turn_u[0, low : low + 1], turn_u[1, low : low + 1]
            parts.append((re * cos + im * sin, im * cos - re * sin))
        for part, (re, im) in enumerate(fft_points(parts, -1.0)):
            pr, pi = (pupil[c, part, half * 8 : half * 8 + 8] for c in range(2))
            grad_out[half, part, 0] = pr * re + pi * im
            grad_out[half, part, 1] = pr * im - pi * re
        send_half(led_axis, half, *grad_refs)

    wait_sent(led_axis, *led_refs)
    wait_sent(tile_axis, *tile_refs)
    wait_sent(tile_axis, *back_refs)
    for half in range(2):
        wait_half(led_axis, half, *grad_refs)
        out_ref[half] = grad_in[half]
    wait_sent(led_axis, *grad_refs)


def update_kernel(led_ref, row_ref, col_ref, spec_ref, grad_ref, out_ref):
    led_here = lax.axis_index("led")
    tile_here = lax.axis_index("tile")
    out_ref[...] = spec_ref[...]

    @pl.loop(0, N_LED)
    def _(slot):
        row = window_row(led_ref, row_ref, col_ref, slot, tile_here, led_here)
        for half in range(2):
            for c in range(2):
                span = slice(c * 16 + half * 8, c * 16 + half * 8 + 8)
                out_ref[row, span] = out_ref[row, span] - STEP_SIZE * grad_ref[half, slot, c]


def shards(spectrum, intensities, led_of_slot, row_offset, col_offset, tile_mask, aberration):
    rows = spectrum.reshape(GR * GC, 2 * LINES, 128)
    masks = jnp.transpose(tile_mask, (1, 2, 0)).reshape(64, N_LED)
    smem = pl.BlockSpec(memory_space=pltpu.SMEM)
    vmem = pl.BlockSpec(memory_space=pltpu.VMEM)
    hbm = pl.BlockSpec(memory_space=pltpu.HBM)
    message = pltpu.VMEM((2, N_LED, 2, 8, 128), jnp.float32)
    band = pltpu.VMEM((2, N_TILE, 2, 8, 256), jnp.float32)
    lines = pltpu.VMEM((256, 256), jnp.bfloat16)
    leds = pltpu.SemaphoreType.DMA((2, N_LED))
    tiles = pltpu.SemaphoreType.DMA((2, N_TILE))
    grad = pl.pallas_call(
        exchange_kernel,
        out_shape=jax.ShapeDtypeStruct((2, N_LED, 2, 8, 128), jnp.float32),
        in_specs=[smem] * 5 + [hbm] * 2,
        out_specs=vmem,
        scratch_shapes=[
            pltpu.VMEM((GR * GC, 2 * LINES, 128), jnp.float32),
            pltpu.VMEM((1, BAND, M), jnp.bfloat16),
            pltpu.VMEM((512, 128), jnp.float32),
            lines,
            lines,
            pltpu.VMEM((2, 32, 128), jnp.float32),
            pltpu.VMEM((2, 64, 8, 128), jnp.float32),
            message,
            message,
            pltpu.VMEM((2, N_LED, 16, 128), jnp.float32),
            pltpu.VMEM((2, 256, 128), jnp.float32),
            lines,
            lines,
            band,
            band,
            pltpu.VMEM((2, 4, 16, 8, 128), jnp.float32),
            band,
            band,
            message,
            message,
            pltpu.SemaphoreType.DMA,
            pltpu.SemaphoreType.DMA,
            leds,
            leds,
            tiles,
            tiles,
            tiles,
            tiles,
            leds,
            leds,
        ],
        compiler_params=pltpu.CompilerParams(
            collective_id=0, has_side_effects=True, vmem_limit_bytes=40 * 1024 * 1024
        ),
    )(led_of_slot, row_offset, col_offset, masks, aberration, rows, intensities)
    updated = pl.pallas_call(
        update_kernel,
        out_shape=jax.ShapeDtypeStruct((GR * GC, 2 * LINES, 128), jnp.float32),
        in_specs=[smem] * 3 + [vmem] * 2,
        out_specs=vmem,
        compiler_params=pltpu.CompilerParams(vmem_limit_bytes=24 * 1024 * 1024),
    )(led_of_slot, row_offset, col_offset, rows, grad)
    return updated.reshape(spectrum.shape)


def solution(mesh):
    placed = (P(None, None, "tile", "led", None), P("led", "tile", None), P(), P(), P(), P(), P())
    return jax.shard_map(
        shards,
        mesh=mesh,
        in_specs=placed,
        out_specs=P(None, None, "tile", "led", None),
        check_vma=False,
    )
```

```python
import math

import jax
import jax.numpy as jnp
from jax import lax
from jax.experimental import pallas as pl
from jax.experimental.pallas import tpu as pltpu
from jax.sharding import PartitionSpec as P

M = 1024
TILE = 128
GR = 16
GC = 8
N_LED = 32
N_TILE = 16
BAND = M // N_TILE
CU = M // N_LED
LINES = BAND * CU // 128
PARTS = 4
STEP_SIZE = 0.25
MESH = pl.DeviceIdType.MESH


def turn(re, im, angle):
    eighth = round(angle / (math.pi / 4.0), 9)
    if eighth == int(eighth) and int(eighth) % 2 == 0:
        quarter = int(eighth) // 2 % 4
        return ((re, im), (-im, re), (-re, -im), (im, -re))[quarter]
    cos, sin = math.cos(angle), math.sin(angle)
    return re * cos - im * sin, im * cos + re * sin


def fft_points(parts, sign):
    count = len(parts)
    if count == 1:
        return list(parts)
    if count == 2:
        (ar, ai), (br, bi) = parts
        return [(ar + br, ai + bi), (ar - br, ai - bi)]
    quarter = count // 4
    subs = [fft_points(parts[r::4], sign) for r in range(4)]
    out = [None] * count
    for k in range(quarter):
        (ar, ai), (br, bi), (cr, ci), (dr, di) = (
            turn(*subs[r][k], sign * 2.0 * math.pi * r * k / count) for r in range(4)
        )
        sr, si, tr, ti = ar + cr, ai + ci, ar - cr, ai - ci
        ur, ui, vr, vi = br + dr, bi + di, br - dr, bi - di
        out[k] = (sr + ur, si + ui)
        out[k + 2 * quarter] = (sr - ur, si - ui)
        if sign > 0:
            out[k + quarter] = (tr - vi, ti + vr)
            out[k + 3 * quarter] = (tr + vi, ti - vr)
        else:
            out[k + quarter] = (tr + vi, ti - vr)
            out[k + 3 * quarter] = (tr - vi, ti + vr)
    return out


def digit(shape, axis, unit):
    return lax.broadcasted_iota(jnp.int32, shape, axis) // unit


def swapped(x, distance, axis):
    size = x.shape[axis]
    if 2 * distance == size:
        return pltpu.roll(x, distance, axis)
    low = digit(x.shape, axis, distance) % 2 == 0
    return jnp.where(low, pltpu.roll(x, size - distance, axis), pltpu.roll(x, distance, axis))


def four_forward(re, im, axis, unit):
    group = digit(re.shape, axis, unit)
    first = jnp.where(group < 2, 1.0, -1.0)
    second = jnp.where(group % 2 == 0, 1.0, -1.0)
    re = first * re + swapped(re, 2 * unit, axis)
    im = first * im + swapped(im, 2 * unit, axis)
    re, im = jnp.where(group == 3, -im, re), jnp.where(group == 3, re, im)
    return second * re + swapped(re, unit, axis), second * im + swapped(im, unit, axis)


def four_backward(re, im, axis, unit):
    group = digit(re.shape, axis, unit)
    first = jnp.where(group < 2, 1.0, -1.0)
    second = jnp.where(group % 2 == 0, 1.0, -1.0)
    re, im = second * re + swapped(re, unit, axis), second * im + swapped(im, unit, axis)
    re, im = jnp.where(group == 3, im, re), jnp.where(group == 3, -re, im)
    return first * re + swapped(re, 2 * unit, axis), first * im + swapped(im, 2 * unit, axis)


def cos_sin(phase):
    count = jnp.floor(phase * (2.0 / math.pi) + 0.5)
    rest = phase - count * 1.5703125
    rest = rest - count * 4.837512969970703125e-4
    rest = rest - count * 7.54978995489188216e-8
    square = rest * rest
    sin_rest = ((-1.9515295891e-4 * square + 8.3321608736e-3) * square - 1.6666654611e-1) * square * rest + rest
    cos_rest = (
        (2.443315711809948e-5 * square - 1.388731625493765e-3) * square + 4.166664568298827e-2
    ) * square * square - 0.5 * square + 1.0
    quadrant = count.astype(jnp.int32) & 3
    odd = (quadrant & 1) == 1
    cos = jnp.where(odd, sin_rest, cos_rest)
    sin = jnp.where(odd, cos_rest, sin_rest)
    cos = jnp.where((quadrant == 1) | (quadrant == 2), -cos, cos)
    return cos, jnp.where(quadrant >= 2, -sin, sin)


def halves(x):
    high = x.astype(jnp.bfloat16)
    return high, (x - high.astype(jnp.float32)).astype(jnp.bfloat16)


def product(left, right, dims):
    def one(a, b):
        return lax.dot_general(a, b, (dims, ((), ())), preferred_element_type=jnp.float32)

    return one(left[0], right[0]) + (one(left[0], right[1]) + one(left[1], right[0]))


def window_row(led_ref, row_ref, col_ref, slot, tile_here, led_here):
    led = led_ref[slot]
    row_start = row_ref[led] * TILE
    col_start = col_ref[led] * TILE
    row_group = (row_start + ((tile_here * BAND - row_start) & (M - 1))) >> 10
    col_group = (col_start + ((led_here * CU - col_start) & (M - 1))) >> 10
    return row_group * GC + col_group


def exchange_kernel(
    led_hbm, row_hbm, col_hbm, mask_hbm, aber_hbm, spec_hbm, image_hbm, grad_hbm,
    led_ref, row_ref, col_ref, mask_ref, aber_ref, spec, measured,
    image, table_hi, table_lo, turn_u, turn_j,
    outgoing, window, pupil, lines, lines_hi, lines_lo, bands_out, bands_in, cells, back_out, back_in,
    grad_out, load_sem, own_sem,
    led_send, led_recv, tile_send, tile_recv, back_send, back_recv, grad_send, grad_recv,
):
    led_here = lax.axis_index("led")
    tile_here = lax.axis_index("tile")
    barrier = pltpu.get_barrier_semaphore()

    def far_first(step, count, here):
        away = step // 2
        return (here + count // 2 + jnp.where(step % 2 == 1, away, -away)) % count

    @pl.loop(1, N_LED)
    def _(step):
        peer = far_first(step, N_LED, led_here)
        pl.semaphore_signal(barrier, inc=1, device_id={"led": peer}, device_id_type=MESH)

    loads = [
        pltpu.make_async_copy(src, dst, load_sem.at[k])
        for k, (src, dst) in enumerate(
            (
                (led_hbm, led_ref), (row_hbm, row_ref), (col_hbm, col_ref), (mask_hbm, mask_ref),
                (aber_hbm, aber_ref), (spec_hbm, spec), (image_hbm, measured),
            )
        )
    ]
    for load in loads:
        load.start()

    @pl.loop(1, N_TILE)
    def _(step):
        peer = far_first(step, N_TILE, tile_here)
        pl.semaphore_signal(barrier, inc=1, device_id={"tile": peer}, device_id_type=MESH)

    def target(peer, count, here):
        return (here + 1) % count if isinstance(peer, pl.Slice) else peer

    def led_copy(src, dst, sends, recvs, part, peer, origin):
        return pltpu.make_async_remote_copy(
            src_ref=src.at[part, peer], dst_ref=dst.at[part, origin],
            send_sem=sends.at[part], recv_sem=recvs.at[part],
            device_id={"led": target(peer, N_LED, led_here)}, device_id_type=MESH,
        )

    def tile_copy(src, dst, sends, recvs, part, peer, origin):
        return pltpu.make_async_remote_copy(
            src_ref=src.at[part, peer], dst_ref=dst.at[part, origin],
            send_sem=sends.at[part], recv_sem=recvs.at[part],
            device_id={"tile": target(peer, N_TILE, tile_here)}, device_id_type=MESH,
        )

    led_axis = (led_copy, N_LED, led_here)
    tile_axis = (tile_copy, N_TILE, tile_here)

    def send_part(axis, part, src, dst, sends, recvs):
        copy, count, here = axis

        @pl.loop(1, count)
        def _(step):
            copy(src, dst, sends, recvs, part, far_first(step, count, here), here).start()

    def all_copies(axis, part, src, dst, sends, recvs):
        copy, count, here = axis
        peers = pl.ds(0, count - 1)
        return copy(src, dst, sends, recvs, part, peers, peers)

    def wait_part(axis, part, *refs):
        all_copies(axis, part, *refs).wait_recv()

    def wait_sent(axis, *refs):
        for part in range(PARTS):
            all_copies(axis, part, *refs).wait_send()

    for load in loads:
        load.wait()

    @pl.loop(0, N_LED)
    def _(slot):
        row = window_row(led_ref, row_ref, col_ref, slot, tile_here, led_here)
        for part in range(PARTS):
            for c in range(2):
                outgoing[part, slot, 4 * c : 4 * c + 4] = spec[row, c * 16 + part * 4 : c * 16 + part * 4 + 4]

    def turns(index, modulus):
        return cos_sin((index & (modulus - 1)).astype(jnp.float32) * (2.0 * math.pi / modulus))

    def iota(shape, axis):
        return lax.broadcasted_iota(jnp.int32, shape, axis)

    @pl.loop(0, 8)
    def _(chunk):
        start = pl.multiple_of(chunk * 32, 32)
        rank = start + iota((32, 256), 0)
        entry = iota((32, 256), 1)
        cos, sin = turns((2 * (rank >> 4) + (rank & 1)) * (entry & 31), 32)
        out_im, in_im = (rank >> 3) & 1, entry >> 7
        value = jnp.where(out_im == in_im, cos, jnp.where(out_im == 0, -sin, sin))
        value = jnp.where(((rank >> 1) & 3) == ((entry >> 5) & 3), value * (1.0 / M), 0.0)
        high, low = halves(value)
        table_hi[pl.ds(start, 32), :] = high
        table_lo[pl.ds(start, 32), :] = low

    lane8 = iota((8, 128), 1)
    sub8 = iota((8, 128), 0)
    turn_u[0], turn_u[1] = turns(iota((32, 128), 0) * (iota((32, 128), 1) & 31), M)

    @pl.loop(0, 64)
    def _(low):
        turn_j[0, low], turn_j[1, low] = turns(low * (4 * (lane8 >> 5) + (sub8 >> 1)), M)

    chunk8 = lane8 >> 5
    frequency8 = jnp.where(chunk8 == 1, 2, jnp.where(chunk8 == 2, 1, chunk8))
    turn_hr, turn_hi = turns((sub8 >> 1) * frequency8, 16)

    led = led_ref[led_here]
    row_start = row_ref[led] * TILE
    col_start = col_ref[led] * TILE
    lane = iota((16, 128), 1)
    row_first = (tile_here * BAND - row_start) & (M - 1)
    row_window = row_first + 4 * iota((16, 128), 0) + (lane >> 5)
    coord_p = (row_window - M // 2).astype(jnp.float32) * (1.0 / (M // 2))

    @pl.loop(0, N_LED)
    def _(origin):
        col_first = (origin * CU - col_start) & (M - 1)
        coord_q = (col_first + (lane & 31) - M // 2).astype(jnp.float32) * (1.0 / (M // 2))
        radial = coord_p * coord_p + coord_q * coord_q
        phase = (
            aber_ref[0] * (2.0 * radial - 1.0)
            + aber_ref[1] * (coord_p * coord_p - coord_q * coord_q)
            + aber_ref[2] * (2.0 * coord_p * coord_q)
            + aber_ref[3] * ((3.0 * radial - 2.0) * coord_p)
            + aber_ref[4] * ((3.0 * radial - 2.0) * coord_q)
        )
        gate = mask_ref[(row_first >> 7) * 8 + (col_first >> 7), led].astype(jnp.float32)
        cos, sin = cos_sin(phase)
        for part in range(PARTS):
            pupil[part, origin, 0:4] = gate * cos[part * 4 : part * 4 + 4]
            pupil[part, origin, 4:8] = gate * sin[part * 4 : part * 4 + 4]

    pl.semaphore_wait(barrier, N_LED + N_TILE - 2)

    led_refs = (outgoing, window, led_send, led_recv)
    for part in range(PARTS):
        send_part(led_axis, part, *led_refs)
        window[part, led_here] = outgoing[part, led_here]

    chunk64 = iota((64, 128), 1) >> 5
    for h in range(4):
        pieces = []
        for block in (2 * h, 2 * h + 1):
            lines_here = measured[0, :, block * 128 : block * 128 + 128].astype(jnp.float32)
            turned = jnp.transpose(jnp.concatenate([lines_here, lines_here], axis=0))
            rolled = pltpu.roll(turned, 32, 1)
            pieces += [(turned[f : f + 64], rolled[f : f + 64]) for f in (0, 64)]
        for s in range(2):
            merged = pieces[0][s]
            for m, f in ((1, 2), (2, 1), (3, 3)):
                merged = jnp.where(chunk64 == m, pieces[f][(m + s) % 2], merged)
            image[pl.ds((0, 2, 1, 3)[h] * 2 + s, 64, stride=8), :] = merged

    tile_refs = (bands_out, bands_in, tile_send, tile_recv)
    table = (table_hi[...], table_lo[...])
    for part in range(PARTS):
        wait_part(led_axis, part, *led_refs)
        points = []
        for origin in range(N_LED):
            pr, pi = pupil[part, origin, 0:4], pupil[part, origin, 4:8]
            wr, wi = window[part, origin, 0:4], window[part, origin, 4:8]
            points.append((pr * wr - pi * wi, pr * wi + pi * wr))
        for low, (re, im) in enumerate(fft_points(points, 1.0)):
            cos, sin = turn_u[0, low : low + 1], turn_u[1, low : low + 1]
            lines[0, low * 4 : low * 4 + 4] = re * cos - im * sin
            lines[1, low * 4 : low * 4 + 4] = im * cos + re * sin
        for line in range(4):
            for c in range(2):
                high, low = halves(lines[c, pl.ds(line, 32, stride=4)])
                lines_hi[line * 32 : line * 32 + 32, c * 128 : c * 128 + 128] = high
                lines_lo[line * 32 : line * 32 + 32, c * 128 : c * 128 + 128] = low
        mixed = product(table, (lines_hi[...], lines_lo[...]), ((1,), (1,)))
        bands_out[part] = mixed.reshape(N_TILE, 2, 8, 128)
        send_part(tile_axis, part, *tile_refs)
        bands_in[part, tile_here] = bands_out[part, tile_here]

    for part in range(PARTS):
        wait_part(tile_axis, part, *tile_refs)
        points = fft_points([(bands_in[part, k, 0], bands_in[part, k, 1]) for k in range(N_TILE)], 1.0)
        for low, (re, im) in enumerate(points):
            cells[0, part, low], cells[1, part, low] = turn(re, im, 2.0 * math.pi * low * part / 64)

    @pl.loop(0, 4)
    def _(chunk):
        span = pl.ds(chunk * 4, 4)
        quads = fft_points([(cells[0, q, span], cells[1, q, span]) for q in range(4)], 1.0)
        back = []
        for q, (re, im) in enumerate(quads):
            where = pl.ds(16 * q + chunk * 4, 4)
            jr, ji = turn_j[0, where], turn_j[1, where]
            hr, hi = turn_hr[None], turn_hi[None]
            re, im = re * jr - im * ji, im * jr + re * ji
            re, im = four_forward(re, im, 2, 32)
            re, im = re * hr - im * hi, im * hr + re * hi
            re, im = four_forward(re, im, 1, 2)
            seen = image[pl.ds(pl.multiple_of((16 * q + chunk * 4) * 8, 32), 32), :].reshape(4, 8, 128)
            excess = re * re + im * im - seen
            re, im = excess * re, excess * im
            re, im = four_backward(re, im, 1, 2)
            re, im = re * hr + im * hi, im * hr - re * hi
            re, im = four_backward(re, im, 2, 32)
            back.append((re * jr + im * ji, im * jr - re * ji))
        for q, (re, im) in enumerate(fft_points(back, -1.0)):
            cells[0, q, span] = re
            cells[1, q, span] = im

    back_refs = (back_out, back_in, back_send, back_recv)
    for part in range(PARTS):
        points = [
            turn(cells[0, part, low], cells[1, part, low], -2.0 * math.pi * low * part / 64) for low in range(16)
        ]
        for k, (re, im) in enumerate(fft_points(points, -1.0)):
            back_out[part, k, 0] = re
            back_out[part, k, 1] = im
        send_part(tile_axis, part, *back_refs)
        back_in[part, tile_here] = back_out[part, tile_here]

    grad_refs = (grad_out, grad_hbm, grad_send, grad_recv)
    own = []
    for part in range(PARTS):
        wait_part(tile_axis, part, *back_refs)
        mixed = product(halves(back_in[part].reshape(256, 128)), table, ((0,), (0,)))
        lines[0] = mixed[:, 0:128]
        lines[1] = mixed[:, 128:256]
        points = []
        for low in range(N_LED):
            re, im = (lines[c, pl.ds(low, 4, stride=32)] for c in range(2))
            cos, sin = turn_u[0, low : low + 1], turn_u[1, low : low + 1]
            points.append((re * cos + im * sin, im * cos - re * sin))
        for origin, (re, im) in enumerate(fft_points(points, -1.0)):
            pr, pi = pupil[part, origin, 0:4], pupil[part, origin, 4:8]
            grad_out[part, origin, 0:4] = pr * re + pi * im
            grad_out[part, origin, 4:8] = pr * im - pi * re
        send_part(led_axis, part, *grad_refs)
        own.append(
            pltpu.make_async_copy(grad_out.at[part, led_here], grad_hbm.at[part, led_here], own_sem.at[part])
        )
        own[-1].start()

    wait_sent(led_axis, *led_refs)
    wait_sent(tile_axis, *tile_refs)
    wait_sent(tile_axis, *back_refs)
    for part in range(PARTS):
        own[part].wait()
        wait_part(led_axis, part, *grad_refs)
    wait_sent(led_axis, *grad_refs)


def update_kernel(led_ref, row_ref, col_ref, spec_ref, grad_ref, out_ref):
    led_here = lax.axis_index("led")
    tile_here = lax.axis_index("tile")
    out_ref[...] = spec_ref[...]
    low = lax.broadcasted_iota(jnp.int32, (8, 128), 0) < 4

    @pl.loop(0, N_LED)
    def _(slot):
        row = window_row(led_ref, row_ref, col_ref, slot, tile_here, led_here)
        for half in range(2):
            first, second = grad_ref[2 * half, slot], grad_ref[2 * half + 1, slot]
            re = jnp.where(low, first, pltpu.roll(second, 4, 0))
            im = jnp.where(low, pltpu.roll(first, 4, 0), second)
            for c, step in ((0, re), (1, im)):
                span = slice(c * 16 + half * 8, c * 16 + half * 8 + 8)
                out_ref[row, span] = out_ref[row, span] - STEP_SIZE * step


def shards(spectrum, intensities, led_of_slot, row_offset, col_offset, tile_mask, aberration):
    rows = spectrum.reshape(GR * GC, 2 * LINES, 128)
    masks = jnp.transpose(tile_mask, (1, 2, 0)).reshape(64, N_LED)
    smem = pl.BlockSpec(memory_space=pltpu.SMEM)
    vmem = pl.BlockSpec(memory_space=pltpu.VMEM)
    hbm = pl.BlockSpec(memory_space=pltpu.HBM)
    message = pltpu.VMEM((PARTS, N_LED, 8, 128), jnp.float32)
    band = pltpu.VMEM((PARTS, N_TILE, 2, 8, 128), jnp.float32)
    table = pltpu.VMEM((256, 256), jnp.bfloat16)
    lines = pltpu.VMEM((128, 256), jnp.bfloat16)
    sems = pltpu.SemaphoreType.DMA((PARTS,))
    grad = pl.pallas_call(
        exchange_kernel,
        out_shape=jax.ShapeDtypeStruct((PARTS, N_LED, 8, 128), jnp.float32),
        in_specs=[hbm] * 7,
        out_specs=hbm,
        scratch_shapes=[
            pltpu.SMEM((N_LED,), jnp.int32),
            pltpu.SMEM((N_LED,), jnp.int32),
            pltpu.SMEM((N_LED,), jnp.int32),
            pltpu.SMEM((64, N_LED), jnp.int32),
            pltpu.SMEM((5,), jnp.float32),
            pltpu.VMEM((GR * GC, 2 * LINES, 128), jnp.float32),
            pltpu.VMEM((1, BAND, M), jnp.bfloat16),
            pltpu.VMEM((512, 128), jnp.float32),
            table,
            table,
            pltpu.VMEM((2, 32, 128), jnp.float32),
            pltpu.VMEM((2, 64, 8, 128), jnp.float32),
            message,
            message,
            message,
            pltpu.VMEM((2, 128, 128), jnp.float32),
            lines,
            lines,
            band,
            band,
            pltpu.VMEM((2, PARTS, 16, 8, 128), jnp.float32),
            band,
            band,
            message,
            pltpu.SemaphoreType.DMA((7,)),
            pltpu.SemaphoreType.DMA((PARTS,)),
        ]
        + [sems] * 8,
        compiler_params=pltpu.CompilerParams(
            collective_id=0, has_side_effects=True, vmem_limit_bytes=60 * 1024 * 1024
        ),
    )(led_of_slot, row_offset, col_offset, masks, aberration, rows, intensities)
    updated = pl.pallas_call(
        update_kernel,
        out_shape=jax.ShapeDtypeStruct((GR * GC, 2 * LINES, 128), jnp.float32),
        in_specs=[smem] * 3 + [vmem] * 2,
        out_specs=vmem,
        compiler_params=pltpu.CompilerParams(vmem_limit_bytes=60 * 1024 * 1024),
    )(led_of_slot, row_offset, col_offset, rows, grad)
    return updated.reshape(spectrum.shape)


def solution(mesh):
    placed = (P(None, None, "tile", "led", None), P("led", "tile", None), P(), P(), P(), P(), P())
    return jax.shard_map(
        shards,
        mesh=mesh,
        in_specs=placed,
        out_specs=P(None, None, "tile", "led", None),
        check_vma=False,
    )
```

```python
import math

import jax
import jax.numpy as jnp
from jax import lax
from jax.experimental import pallas as pl
from jax.experimental.pallas import tpu as pltpu
from jax.sharding import PartitionSpec as P

M = 1024
TILE = 128
GR = 16
GC = 8
N_LED = 32
N_TILE = 16
BAND = M // N_TILE
CU = M // N_LED
LINES = BAND * CU // 128
PARTS = 4
STEP_SIZE = 0.25
MESH = pl.DeviceIdType.MESH


def turn(re, im, angle):
    eighth = round(angle / (math.pi / 4.0), 9)
    if eighth == int(eighth) and int(eighth) % 2 == 0:
        quarter = int(eighth) // 2 % 4
        return ((re, im), (-im, re), (-re, -im), (im, -re))[quarter]
    cos, sin = math.cos(angle), math.sin(angle)
    return re * cos - im * sin, im * cos + re * sin


def fft_points(parts, sign):
    count = len(parts)
    if count == 1:
        return list(parts)
    if count == 2:
        (ar, ai), (br, bi) = parts
        return [(ar + br, ai + bi), (ar - br, ai - bi)]
    quarter = count // 4
    subs = [fft_points(parts[r::4], sign) for r in range(4)]
    out = [None] * count
    for k in range(quarter):
        (ar, ai), (br, bi), (cr, ci), (dr, di) = (
            turn(*subs[r][k], sign * 2.0 * math.pi * r * k / count) for r in range(4)
        )
        sr, si, tr, ti = ar + cr, ai + ci, ar - cr, ai - ci
        ur, ui, vr, vi = br + dr, bi + di, br - dr, bi - di
        out[k] = (sr + ur, si + ui)
        out[k + 2 * quarter] = (sr - ur, si - ui)
        if sign > 0:
            out[k + quarter] = (tr - vi, ti + vr)
            out[k + 3 * quarter] = (tr + vi, ti - vr)
        else:
            out[k + quarter] = (tr + vi, ti - vr)
            out[k + 3 * quarter] = (tr - vi, ti + vr)
    return out


def trade_bit(parts, bit, axis, unit):
    size = parts[0].shape[axis]
    clear = (lax.broadcasted_iota(jnp.int32, parts[0].shape, axis) // unit) % 2 == 0
    out = list(parts)
    for low in range(len(parts)):
        if low & bit == 0:
            a, b = parts[low], parts[low | bit]
            out[low] = jnp.where(clear, a, pltpu.roll(b, unit, axis))
            out[low | bit] = jnp.where(clear, pltpu.roll(a, size - unit, axis), b)
    return out


def trade(points, axis, unit):
    halves_here = []
    for parts in zip(*points):
        parts = trade_bit(list(parts), 2, axis, 2 * unit)
        halves_here.append(trade_bit(parts, 1, axis, unit))
    return list(zip(*halves_here))


def cos_sin(phase):
    count = jnp.floor(phase * (2.0 / math.pi) + 0.5)
    rest = phase - count * 1.5703125
    rest = rest - count * 4.837512969970703125e-4
    rest = rest - count * 7.54978995489188216e-8
    square = rest * rest
    sin_rest = ((-1.9515295891e-4 * square + 8.3321608736e-3) * square - 1.6666654611e-1) * square * rest + rest
    cos_rest = (
        (2.443315711809948e-5 * square - 1.388731625493765e-3) * square + 4.166664568298827e-2
    ) * square * square - 0.5 * square + 1.0
    quadrant = count.astype(jnp.int32) & 3
    odd = (quadrant & 1) == 1
    cos = jnp.where(odd, sin_rest, cos_rest)
    sin = jnp.where(odd, cos_rest, sin_rest)
    cos = jnp.where((quadrant == 1) | (quadrant == 2), -cos, cos)
    return cos, jnp.where(quadrant >= 2, -sin, sin)


def halves(x):
    high = x.astype(jnp.bfloat16)
    return high, (x - high.astype(jnp.float32)).astype(jnp.bfloat16)


def product(left, right, dims):
    def one(a, b):
        return lax.dot_general(a, b, (dims, ((), ())), preferred_element_type=jnp.float32)

    return one(left[0], right[0]) + (one(left[0], right[1]) + one(left[1], right[0]))


def window_row(led_ref, row_ref, col_ref, slot, tile_here, led_here):
    led = led_ref[slot]
    row_start = row_ref[led] * TILE
    col_start = col_ref[led] * TILE
    row_group = (row_start + ((tile_here * BAND - row_start) & (M - 1))) >> 10
    col_group = (col_start + ((led_here * CU - col_start) & (M - 1))) >> 10
    return row_group * GC + col_group


def exchange_kernel(
    led_hbm, row_hbm, col_hbm, mask_hbm, aber_hbm, spec_hbm, image_hbm, grad_hbm,
    led_ref, row_ref, col_ref, mask_ref, aber_ref, spec, measured,
    image, table_hi, table_lo, turn_u, turn_j,
    outgoing, window, pupil, lines, lines_hi, lines_lo, bands_out, bands_in, cells, back_out, back_in,
    grad_out, load_sem, own_sem,
    led_send, led_recv, tile_send, tile_recv, back_send, back_recv, grad_send, grad_recv,
):
    led_here = lax.axis_index("led")
    tile_here = lax.axis_index("tile")
    barrier = pltpu.get_barrier_semaphore()

    def far_first(step, count, here):
        away = step // 2
        return (here + count // 2 + jnp.where(step % 2 == 1, away, -away)) % count

    @pl.loop(1, N_LED)
    def _(step):
        peer = far_first(step, N_LED, led_here)
        pl.semaphore_signal(barrier, inc=1, device_id={"led": peer}, device_id_type=MESH)

    loads = [
        pltpu.make_async_copy(src, dst, load_sem.at[k])
        for k, (src, dst) in enumerate(
            (
                (led_hbm, led_ref), (row_hbm, row_ref), (col_hbm, col_ref), (mask_hbm, mask_ref),
                (aber_hbm, aber_ref), (spec_hbm, spec), (image_hbm, measured),
            )
        )
    ]
    for load in loads:
        load.start()

    @pl.loop(1, N_TILE)
    def _(step):
        peer = far_first(step, N_TILE, tile_here)
        pl.semaphore_signal(barrier, inc=1, device_id={"tile": peer}, device_id_type=MESH)

    def target(peer, count, here):
        return (here + 1) % count if isinstance(peer, pl.Slice) else peer

    def led_copy(src, dst, sends, recvs, part, peer, origin):
        return pltpu.make_async_remote_copy(
            src_ref=src.at[part, peer], dst_ref=dst.at[part, origin],
            send_sem=sends.at[part], recv_sem=recvs.at[part],
            device_id={"led": target(peer, N_LED, led_here)}, device_id_type=MESH,
        )

    def tile_copy(src, dst, sends, recvs, part, peer, origin):
        return pltpu.make_async_remote_copy(
            src_ref=src.at[part, peer], dst_ref=dst.at[part, origin],
            send_sem=sends.at[part], recv_sem=recvs.at[part],
            device_id={"tile": target(peer, N_TILE, tile_here)}, device_id_type=MESH,
        )

    led_axis = (led_copy, N_LED, led_here)
    tile_axis = (tile_copy, N_TILE, tile_here)

    def send_part(axis, part, src, dst, sends, recvs):
        copy, count, here = axis

        @pl.loop(1, count)
        def _(step):
            copy(src, dst, sends, recvs, part, far_first(step, count, here), here).start()

    def all_copies(axis, part, src, dst, sends, recvs):
        copy, count, here = axis
        peers = pl.ds(0, count - 1)
        return copy(src, dst, sends, recvs, part, peers, peers)

    def wait_part(axis, part, *refs):
        all_copies(axis, part, *refs).wait_recv()

    def wait_sent(axis, *refs):
        for part in range(PARTS):
            all_copies(axis, part, *refs).wait_send()

    for load in loads:
        load.wait()

    @pl.loop(0, N_LED)
    def _(slot):
        row = window_row(led_ref, row_ref, col_ref, slot, tile_here, led_here)
        for part in range(PARTS):
            for c in range(2):
                outgoing[part, slot, 4 * c : 4 * c + 4] = spec[row, c * 16 + part * 4 : c * 16 + part * 4 + 4]

    pl.semaphore_wait(barrier, N_LED + N_TILE - 2)

    led_refs = (outgoing, window, led_send, led_recv)
    for part in range(PARTS):
        send_part(led_axis, part, *led_refs)
        window[part, led_here] = outgoing[part, led_here]

    def turns(index, modulus):
        return cos_sin((index & (modulus - 1)).astype(jnp.float32) * (2.0 * math.pi / modulus))

    def iota(shape, axis):
        return lax.broadcasted_iota(jnp.int32, shape, axis)

    @pl.loop(0, 8)
    def _(chunk):
        start = pl.multiple_of(chunk * 32, 32)
        rank = start + iota((32, 256), 0)
        entry = iota((32, 256), 1)
        cos, sin = turns((2 * (rank >> 4) + (rank & 1)) * (entry & 31), 32)
        out_im, in_im = (rank >> 3) & 1, entry >> 7
        value = jnp.where(out_im == in_im, cos, jnp.where(out_im == 0, -sin, sin))
        value = jnp.where(((rank >> 1) & 3) == ((entry >> 5) & 3), value * (1.0 / M), 0.0)
        high, low = halves(value)
        table_hi[pl.ds(start, 32), :] = high
        table_lo[pl.ds(start, 32), :] = low

    lane8 = iota((8, 128), 1)
    sub8 = iota((8, 128), 0)
    turn_u[0], turn_u[1] = turns(iota((32, 128), 0) * (iota((32, 128), 1) & 31), M)

    @pl.loop(0, 64)
    def _(low):
        turn_j[0, low], turn_j[1, low] = turns(low * (4 * (lane8 >> 5) + (sub8 >> 1)), M)

    turn_h = [turns((sub8 >> 1) * f, 16) for f in range(4)]

    led = led_ref[led_here]
    row_start = row_ref[led] * TILE
    col_start = col_ref[led] * TILE
    lane = iota((16, 128), 1)
    row_first = (tile_here * BAND - row_start) & (M - 1)
    row_window = row_first + 4 * iota((16, 128), 0) + (lane >> 5)
    coord_p = (row_window - M // 2).astype(jnp.float32) * (1.0 / (M // 2))

    @pl.loop(0, N_LED)
    def _(origin):
        col_first = (origin * CU - col_start) & (M - 1)
        coord_q = (col_first + (lane & 31) - M // 2).astype(jnp.float32) * (1.0 / (M // 2))
        radial = coord_p * coord_p + coord_q * coord_q
        phase = (
            aber_ref[0] * (2.0 * radial - 1.0)
            + aber_ref[1] * (coord_p * coord_p - coord_q * coord_q)
            + aber_ref[2] * (2.0 * coord_p * coord_q)
            + aber_ref[3] * ((3.0 * radial - 2.0) * coord_p)
            + aber_ref[4] * ((3.0 * radial - 2.0) * coord_q)
        )
        gate = mask_ref[(row_first >> 7) * 8 + (col_first >> 7), led].astype(jnp.float32)
        cos, sin = cos_sin(phase)
        for part in range(PARTS):
            pupil[part, origin, 0:4] = gate * cos[part * 4 : part * 4 + 4]
            pupil[part, origin, 4:8] = gate * sin[part * 4 : part * 4 + 4]

    chunk16 = iota((16, 128), 1) >> 5
    for block in range(8):
        lines_here = measured[0, :, block * 128 : block * 128 + 128].astype(jnp.float32)
        turned = jnp.transpose(jnp.concatenate([lines_here, lines_here], axis=0))
        sides = (turned, pltpu.roll(turned, 32, 1))
        for odd in range(2):
            f = 2 * (block % 2) + odd
            for s in range(2):
                pieces = [sides[(g + s) % 2][odd * 64 + g * 16 : odd * 64 + g * 16 + 16] for g in range(4)]
                merged = pieces[0]
                for g in range(1, 4):
                    merged = jnp.where(chunk16 == g, pieces[g], merged)
                image[pl.ds((block // 2) * 128 + 2 * f + s, 16, stride=8), :] = merged

    tile_refs = (bands_out, bands_in, tile_send, tile_recv)
    table = (table_hi[...], table_lo[...])
    for part in range(PARTS):
        wait_part(led_axis, part, *led_refs)
        points = []
        for origin in range(N_LED):
            pr, pi = pupil[part, origin, 0:4], pupil[part, origin, 4:8]
            wr, wi = window[part, origin, 0:4], window[part, origin, 4:8]
            points.append((pr * wr - pi * wi, pr * wi + pi * wr))
        for low, (re, im) in enumerate(fft_points(points, 1.0)):
            cos, sin = turn_u[0, low : low + 1], turn_u[1, low : low + 1]
            lines[0, low * 4 : low * 4 + 4] = re * cos - im * sin
            lines[1, low * 4 : low * 4 + 4] = im * cos + re * sin
        for line in range(4):
            for c in range(2):
                high, low = halves(lines[c, pl.ds(line, 32, stride=4)])
                lines_hi[line * 32 : line * 32 + 32, c * 128 : c * 128 + 128] = high
                lines_lo[line * 32 : line * 32 + 32, c * 128 : c * 128 + 128] = low
        mixed = product(table, (lines_hi[...], lines_lo[...]), ((1,), (1,)))
        bands_out[part] = mixed.reshape(N_TILE, 2, 8, 128)
        send_part(tile_axis, part, *tile_refs)
        bands_in[part, tile_here] = bands_out[part, tile_here]

    for part in range(PARTS):
        wait_part(tile_axis, part, *tile_refs)
        points = fft_points([(bands_in[part, k, 0], bands_in[part, k, 1]) for k in range(N_TILE)], 1.0)
        for low, (re, im) in enumerate(points):
            cells[0, part, low], cells[1, part, low] = turn(re, im, 2.0 * math.pi * low * part / 64)

    @pl.loop(0, 4)
    def _(chunk):
        span = pl.ds(chunk * 4, 4)
        tables = [(turn_j[0, where], turn_j[1, where]) for where in (pl.ds(16 * g + chunk * 4, 4) for g in range(4))]
        points = fft_points([(cells[0, q, span], cells[1, q, span]) for q in range(4)], 1.0)
        points = [(re * c - im * s, im * c + re * s) for (re, im), (c, s) in zip(points, tables)]
        points = fft_points(trade(points, 2, 32), 1.0)
        points = [(re * c - im * s, im * c + re * s) for (re, im), (c, s) in zip(points, turn_h)]
        points = fft_points(trade(points, 1, 2), 1.0)
        excess = []
        for h, (re, im) in enumerate(points):
            start = pl.multiple_of((16 * h + chunk * 4) * 8, 32)
            rest = re * re + im * im - image[pl.ds(start, 32), :].reshape(4, 8, 128)
            excess.append((rest * re, rest * im))
        points = trade(fft_points(excess, -1.0), 1, 2)
        points = [(re * c + im * s, im * c - re * s) for (re, im), (c, s) in zip(points, turn_h)]
        points = trade(fft_points(points, -1.0), 2, 32)
        points = [(re * c + im * s, im * c - re * s) for (re, im), (c, s) in zip(points, tables)]
        for q, (re, im) in enumerate(fft_points(points, -1.0)):
            cells[0, q, span] = re
            cells[1, q, span] = im

    back_refs = (back_out, back_in, back_send, back_recv)
    for part in range(PARTS):
        points = [
            turn(cells[0, part, low], cells[1, part, low], -2.0 * math.pi * low * part / 64) for low in range(16)
        ]
        for k, (re, im) in enumerate(fft_points(points, -1.0)):
            back_out[part, k, 0] = re
            back_out[part, k, 1] = im
        send_part(tile_axis, part, *back_refs)
        back_in[part, tile_here] = back_out[part, tile_here]

    grad_refs = (grad_out, grad_hbm, grad_send, grad_recv)
    own = []
    for part in range(PARTS):
        wait_part(tile_axis, part, *back_refs)
        mixed = product(halves(back_in[part].reshape(256, 128)), table, ((0,), (0,)))
        lines[0] = mixed[:, 0:128]
        lines[1] = mixed[:, 128:256]
        points = []
        for low in range(N_LED):
            re, im = (lines[c, pl.ds(low, 4, stride=32)] for c in range(2))
            cos, sin = turn_u[0, low : low + 1], turn_u[1, low : low + 1]
            points.append((re * cos + im * sin, im * cos - re * sin))
        for origin, (re, im) in enumerate(fft_points(points, -1.0)):
            pr, pi = pupil[part, origin, 0:4], pupil[part, origin, 4:8]
            grad_out[part, origin, 0:4] = pr * re + pi * im
            grad_out[part, origin, 4:8] = pr * im - pi * re
        send_part(led_axis, part, *grad_refs)
        own.append(
            pltpu.make_async_copy(grad_out.at[part, led_here], grad_hbm.at[part, led_here], own_sem.at[part])
        )
        own[-1].start()

    wait_sent(led_axis, *led_refs)
    wait_sent(tile_axis, *tile_refs)
    wait_sent(tile_axis, *back_refs)
    for part in range(PARTS):
        own[part].wait()
        wait_part(led_axis, part, *grad_refs)
    wait_sent(led_axis, *grad_refs)


def update_kernel(
    led_hbm, row_hbm, col_hbm, spec_hbm, grad_hbm, out_hbm, led_ref, row_ref, col_ref, rows_ref, spec, grad,
    load_sem, store_sem,
):
    led_here = lax.axis_index("led")
    tile_here = lax.axis_index("tile")
    sides = [pl.ds(c * 16, 16) for c in range(2)]
    loads = [
        pltpu.make_async_copy(src, dst, load_sem.at[k])
        for k, (src, dst) in enumerate(
            (
                (led_hbm, led_ref), (row_hbm, row_ref), (col_hbm, col_ref), (grad_hbm, grad),
                (spec_hbm.at[:, sides[0]], spec.at[:, sides[0]]), (spec_hbm.at[:, sides[1]], spec.at[:, sides[1]]),
            )
        )
    ]
    for load in loads:
        load.start()
    for load in loads[:3]:
        load.wait()

    @pl.loop(0, N_LED, unroll=4)
    def _(slot):
        rows_ref[slot] = window_row(led_ref, row_ref, col_ref, slot, tile_here, led_here)

    loads[3].wait()
    low = lax.broadcasted_iota(jnp.int32, (8, 128), 0) < 4
    stores = []
    for c in range(2):
        loads[4 + c].wait()

        @pl.loop(0, N_LED, unroll=8)
        def _(slot):
            row = rows_ref[slot]
            for half in range(2):
                first, second = grad[2 * half, slot], grad[2 * half + 1, slot]
                if c == 0:
                    step = jnp.where(low, first, pltpu.roll(second, 4, 0))
                else:
                    step = jnp.where(low, pltpu.roll(first, 4, 0), second)
                span = slice(c * 16 + half * 8, c * 16 + half * 8 + 8)
                spec[row, span] = spec[row, span] - STEP_SIZE * step

        stores.append(pltpu.make_async_copy(spec.at[:, sides[c]], out_hbm.at[:, sides[c]], store_sem.at[c]))
        stores[c].start()
    for store in stores:
        store.wait()


def shards(spectrum, intensities, led_of_slot, row_offset, col_offset, tile_mask, aberration):
    rows = spectrum.reshape(GR * GC, 2 * LINES, 128)
    masks = jnp.transpose(tile_mask, (1, 2, 0)).reshape(64, N_LED)
    hbm = pl.BlockSpec(memory_space=pltpu.HBM)
    message = pltpu.VMEM((PARTS, N_LED, 8, 128), jnp.float32)
    band = pltpu.VMEM((PARTS, N_TILE, 2, 8, 128), jnp.float32)
    table = pltpu.VMEM((256, 256), jnp.bfloat16)
    lines = pltpu.VMEM((128, 256), jnp.bfloat16)
    sems = pltpu.SemaphoreType.DMA((PARTS,))
    grad = pl.pallas_call(
        exchange_kernel,
        out_shape=jax.ShapeDtypeStruct((PARTS, N_LED, 8, 128), jnp.float32),
        in_specs=[hbm] * 7,
        out_specs=hbm,
        scratch_shapes=[
            pltpu.SMEM((N_LED,), jnp.int32),
            pltpu.SMEM((N_LED,), jnp.int32),
            pltpu.SMEM((N_LED,), jnp.int32),
            pltpu.SMEM((64, N_LED), jnp.int32),
            pltpu.SMEM((5,), jnp.float32),
            pltpu.VMEM((GR * GC, 2 * LINES, 128), jnp.float32),
            pltpu.VMEM((1, BAND, M), jnp.bfloat16),
            pltpu.VMEM((512, 128), jnp.float32),
            table,
            table,
            pltpu.VMEM((2, 32, 128), jnp.float32),
            pltpu.VMEM((2, 64, 8, 128), jnp.float32),
            message,
            message,
            message,
            pltpu.VMEM((2, 128, 128), jnp.float32),
            lines,
            lines,
            band,
            band,
            pltpu.VMEM((2, PARTS, 16, 8, 128), jnp.float32),
            band,
            band,
            message,
            pltpu.SemaphoreType.DMA((7,)),
            pltpu.SemaphoreType.DMA((PARTS,)),
        ]
        + [sems] * 8,
        compiler_params=pltpu.CompilerParams(
            collective_id=0, has_side_effects=True, vmem_limit_bytes=60 * 1024 * 1024
        ),
    )(led_of_slot, row_offset, col_offset, masks, aberration, rows, intensities)
    updated = pl.pallas_call(
        update_kernel,
        out_shape=jax.ShapeDtypeStruct((GR * GC, 2 * LINES, 128), jnp.float32),
        in_specs=[hbm] * 5,
        out_specs=hbm,
        scratch_shapes=[
            pltpu.SMEM((N_LED,), jnp.int32),
            pltpu.SMEM((N_LED,), jnp.int32),
            pltpu.SMEM((N_LED,), jnp.int32),
            pltpu.SMEM((N_LED,), jnp.int32),
            pltpu.VMEM((GR * GC, 2 * LINES, 128), jnp.float32),
            message,
            pltpu.SemaphoreType.DMA((6,)),
            pltpu.SemaphoreType.DMA((2,)),
        ],
        compiler_params=pltpu.CompilerParams(vmem_limit_bytes=60 * 1024 * 1024),
    )(led_of_slot, row_offset, col_offset, rows, grad)
    return updated.reshape(spectrum.shape)


def solution(mesh):
    placed = (P(None, None, "tile", "led", None), P("led", "tile", None), P(), P(), P(), P(), P())
    return jax.shard_map(
        shards,
        mesh=mesh,
        in_specs=placed,
        out_specs=P(None, None, "tile", "led", None),
        check_vma=False,
    )
```

```python
import math

import jax
import jax.numpy as jnp
from jax import lax
from jax.experimental import pallas as pl
from jax.experimental.pallas import tpu as pltpu
from jax.sharding import PartitionSpec as P

M = 1024
TILE = 128
GR = 16
GC = 8
N_LED = 32
N_TILE = 16
BAND = M // N_TILE
CU = M // N_LED
LINES = BAND * CU // 128
PARTS = 4
STEP_SIZE = 0.25
MESH = pl.DeviceIdType.MESH


def turn(re, im, angle):
    eighth = round(angle / (math.pi / 4.0), 9)
    if eighth == int(eighth) and int(eighth) % 2 == 0:
        quarter = int(eighth) // 2 % 4
        return ((re, im), (-im, re), (-re, -im), (im, -re))[quarter]
    cos, sin = math.cos(angle), math.sin(angle)
    return re * cos - im * sin, im * cos + re * sin


def fft_points(parts, sign):
    count = len(parts)
    if count == 1:
        return list(parts)
    if count == 2:
        (ar, ai), (br, bi) = parts
        return [(ar + br, ai + bi), (ar - br, ai - bi)]
    quarter = count // 4
    subs = [fft_points(parts[r::4], sign) for r in range(4)]
    out = [None] * count
    for k in range(quarter):
        (ar, ai), (br, bi), (cr, ci), (dr, di) = (
            turn(*subs[r][k], sign * 2.0 * math.pi * r * k / count) for r in range(4)
        )
        sr, si, tr, ti = ar + cr, ai + ci, ar - cr, ai - ci
        ur, ui, vr, vi = br + dr, bi + di, br - dr, bi - di
        out[k] = (sr + ur, si + ui)
        out[k + 2 * quarter] = (sr - ur, si - ui)
        if sign > 0:
            out[k + quarter] = (tr - vi, ti + vr)
            out[k + 3 * quarter] = (tr + vi, ti - vr)
        else:
            out[k + quarter] = (tr + vi, ti - vr)
            out[k + 3 * quarter] = (tr - vi, ti + vr)
    return out


def trade_bit(parts, bit, axis, unit):
    size = parts[0].shape[axis]
    clear = (lax.broadcasted_iota(jnp.int32, parts[0].shape, axis) // unit) % 2 == 0
    out = list(parts)
    for low in range(len(parts)):
        if low & bit == 0:
            a, b = parts[low], parts[low | bit]
            out[low] = jnp.where(clear, a, pltpu.roll(b, unit, axis))
            out[low | bit] = jnp.where(clear, pltpu.roll(a, size - unit, axis), b)
    return out


def trade(points, axis, unit):
    halves_here = []
    for parts in zip(*points):
        parts = trade_bit(list(parts), 2, axis, 2 * unit)
        halves_here.append(trade_bit(parts, 1, axis, unit))
    return list(zip(*halves_here))


def cos_sin(phase):
    count = jnp.floor(phase * (2.0 / math.pi) + 0.5)
    rest = phase - count * 1.5703125
    rest = rest - count * 4.837512969970703125e-4
    rest = rest - count * 7.54978995489188216e-8
    square = rest * rest
    sin_rest = ((-1.9515295891e-4 * square + 8.3321608736e-3) * square - 1.6666654611e-1) * square * rest + rest
    cos_rest = (
        (2.443315711809948e-5 * square - 1.388731625493765e-3) * square + 4.166664568298827e-2
    ) * square * square - 0.5 * square + 1.0
    quadrant = count.astype(jnp.int32) & 3
    odd = (quadrant & 1) == 1
    cos = jnp.where(odd, sin_rest, cos_rest)
    sin = jnp.where(odd, cos_rest, sin_rest)
    cos = jnp.where((quadrant == 1) | (quadrant == 2), -cos, cos)
    return cos, jnp.where(quadrant >= 2, -sin, sin)


def halves(x):
    high = x.astype(jnp.bfloat16)
    return high, (x - high.astype(jnp.float32)).astype(jnp.bfloat16)


def product(left, right, dims):
    def one(a, b):
        return lax.dot_general(a, b, (dims, ((), ())), preferred_element_type=jnp.float32)

    return one(left[0], right[0]) + (one(left[0], right[1]) + one(left[1], right[0]))


def window_row(led_ref, row_ref, col_ref, slot, tile_here, led_here):
    led = led_ref[slot]
    row_start = row_ref[led] * TILE
    col_start = col_ref[led] * TILE
    row_group = (row_start + ((tile_here * BAND - row_start) & (M - 1))) >> 10
    col_group = (col_start + ((led_here * CU - col_start) & (M - 1))) >> 10
    return row_group * GC + col_group


def exchange_kernel(
    led_hbm, row_hbm, col_hbm, mask_hbm, aber_hbm, spec_hbm, image_hbm, grad_hbm,
    led_ref, row_ref, col_ref, mask_ref, aber_ref, spec, measured,
    image, table_hi, table_lo, turn_u, turn_j,
    outgoing, window, pupil, lines, lines_hi, lines_lo, bands_out, bands_in, cells, back_out, back_in,
    grad_out, load_sem, own_sem,
    led_send, led_recv, tile_send, tile_recv, back_send, back_recv, grad_send, grad_recv,
):
    led_here = lax.axis_index("led")
    tile_here = lax.axis_index("tile")
    barrier = pltpu.get_barrier_semaphore()

    def far_first(step, count, here):
        away = step // 2
        return (here + count // 2 + jnp.where(step % 2 == 1, away, -away)) % count

    @pl.loop(1, N_LED)
    def _(step):
        peer = far_first(step, N_LED, led_here)
        pl.semaphore_signal(barrier, inc=1, device_id={"led": peer}, device_id_type=MESH)

    loads = [
        pltpu.make_async_copy(src, dst, load_sem.at[k])
        for k, (src, dst) in enumerate(
            (
                (led_hbm, led_ref), (row_hbm, row_ref), (col_hbm, col_ref), (mask_hbm, mask_ref),
                (aber_hbm, aber_ref), (spec_hbm, spec), (image_hbm, measured),
            )
        )
    ]
    for load in loads:
        load.start()

    @pl.loop(1, N_TILE)
    def _(step):
        peer = far_first(step, N_TILE, tile_here)
        pl.semaphore_signal(barrier, inc=1, device_id={"tile": peer}, device_id_type=MESH)

    def target(peer, count, here):
        return (here + 1) % count if isinstance(peer, pl.Slice) else peer

    def led_copy(src, dst, sends, recvs, part, peer, origin):
        return pltpu.make_async_remote_copy(
            src_ref=src.at[part, peer], dst_ref=dst.at[part, origin],
            send_sem=sends.at[part], recv_sem=recvs.at[part],
            device_id={"led": target(peer, N_LED, led_here)}, device_id_type=MESH,
        )

    def tile_copy(src, dst, sends, recvs, part, peer, origin):
        return pltpu.make_async_remote_copy(
            src_ref=src.at[part, peer], dst_ref=dst.at[part, origin],
            send_sem=sends.at[part], recv_sem=recvs.at[part],
            device_id={"tile": target(peer, N_TILE, tile_here)}, device_id_type=MESH,
        )

    led_axis = (led_copy, N_LED, led_here)
    tile_axis = (tile_copy, N_TILE, tile_here)

    def send_part(axis, part, src, dst, sends, recvs):
        copy, count, here = axis

        @pl.loop(1, count)
        def _(step):
            copy(src, dst, sends, recvs, part, far_first(step, count, here), here).start()

    def all_copies(axis, part, src, dst, sends, recvs):
        copy, count, here = axis
        peers = pl.ds(0, count - 1)
        return copy(src, dst, sends, recvs, part, peers, peers)

    def wait_part(axis, part, *refs):
        all_copies(axis, part, *refs).wait_recv()

    def wait_sent(axis, *refs):
        for part in range(PARTS):
            all_copies(axis, part, *refs).wait_send()

    for load in loads:
        load.wait()

    @pl.loop(0, N_LED)
    def _(slot):
        row = window_row(led_ref, row_ref, col_ref, slot, tile_here, led_here)
        for part in range(PARTS):
            for c in range(2):
                outgoing[part, slot, 4 * c : 4 * c + 4] = spec[row, c * 16 + part * 4 : c * 16 + part * 4 + 4]

    pl.semaphore_wait(barrier, N_LED + N_TILE - 2)

    led_refs = (outgoing, window, led_send, led_recv)
    for part in range(PARTS):
        send_part(led_axis, part, *led_refs)
        window[part, led_here] = outgoing[part, led_here]

    def turns(index, modulus):
        return cos_sin((index & (modulus - 1)).astype(jnp.float32) * (2.0 * math.pi / modulus))

    def iota(shape, axis):
        return lax.broadcasted_iota(jnp.int32, shape, axis)

    @pl.loop(0, 8)
    def _(chunk):
        start = pl.multiple_of(chunk * 32, 32)
        rank = start + iota((32, 256), 0)
        entry = iota((32, 256), 1)
        cos, sin = turns((2 * (rank >> 4) + (rank & 1)) * (entry & 31), 32)
        out_im, in_im = (rank >> 3) & 1, entry >> 7
        value = jnp.where(out_im == in_im, cos, jnp.where(out_im == 0, -sin, sin))
        value = jnp.where(((rank >> 1) & 3) == ((entry >> 5) & 3), value * (1.0 / M), 0.0)
        high, low = halves(value)
        table_hi[pl.ds(start, 32), :] = high
        table_lo[pl.ds(start, 32), :] = low

    lane8 = iota((8, 128), 1)
    sub8 = iota((8, 128), 0)
    turn_u[0], turn_u[1] = turns(iota((32, 128), 0) * (iota((32, 128), 1) & 31), M)

    @pl.loop(0, 64)
    def _(low):
        turn_j[0, low], turn_j[1, low] = turns(low * (4 * (lane8 >> 5) + (sub8 >> 1)), M)

    turn_h = [turns((sub8 >> 1) * f, 16) for f in range(4)]

    led = led_ref[led_here]
    row_start = row_ref[led] * TILE
    col_start = col_ref[led] * TILE
    lane = iota((16, 128), 1)
    row_first = (tile_here * BAND - row_start) & (M - 1)
    row_window = row_first + 4 * iota((16, 128), 0) + (lane >> 5)
    coord_p = (row_window - M // 2).astype(jnp.float32) * (1.0 / (M // 2))

    @pl.loop(0, N_LED)
    def _(origin):
        col_first = (origin * CU - col_start) & (M - 1)
        coord_q = (col_first + (lane & 31) - M // 2).astype(jnp.float32) * (1.0 / (M // 2))
        radial = coord_p * coord_p + coord_q * coord_q
        phase = (
            aber_ref[0] * (2.0 * radial - 1.0)
            + aber_ref[1] * (coord_p * coord_p - coord_q * coord_q)
            + aber_ref[2] * (2.0 * coord_p * coord_q)
            + aber_ref[3] * ((3.0 * radial - 2.0) * coord_p)
            + aber_ref[4] * ((3.0 * radial - 2.0) * coord_q)
        )
        gate = mask_ref[(row_first >> 7) * 8 + (col_first >> 7), led].astype(jnp.float32)
        cos, sin = cos_sin(phase)
        for part in range(PARTS):
            pupil[part, origin, 0:4] = gate * cos[part * 4 : part * 4 + 4]
            pupil[part, origin, 4:8] = gate * sin[part * 4 : part * 4 + 4]

    chunk16 = iota((16, 128), 1) >> 5
    for block in range(8):
        lines_here = measured[0, :, block * 128 : block * 128 + 128].astype(jnp.float32)
        turned = jnp.transpose(jnp.concatenate([lines_here, lines_here], axis=0))
        sides = (turned, pltpu.roll(turned, 32, 1))
        for odd in range(2):
            f = 2 * (block % 2) + odd
            for s in range(2):
                pieces = [sides[(g + s) % 2][odd * 64 + g * 16 : odd * 64 + g * 16 + 16] for g in range(4)]
                merged = pieces[0]
                for g in range(1, 4):
                    merged = jnp.where(chunk16 == g, pieces[g], merged)
                image[pl.ds((block // 2) * 128 + 2 * f + s, 16, stride=8), :] = merged

    tile_refs = (bands_out, bands_in, tile_send, tile_recv)
    table = (table_hi[...], table_lo[...])
    for part in range(PARTS):
        wait_part(led_axis, part, *led_refs)
        points = []
        for origin in range(N_LED):
            pr, pi = pupil[part, origin, 0:4], pupil[part, origin, 4:8]
            wr, wi = window[part, origin, 0:4], window[part, origin, 4:8]
            points.append((pr * wr - pi * wi, pr * wi + pi * wr))
        for low, (re, im) in enumerate(fft_points(points, 1.0)):
            cos, sin = turn_u[0, low : low + 1], turn_u[1, low : low + 1]
            lines[0, low * 4 : low * 4 + 4] = re * cos - im * sin
            lines[1, low * 4 : low * 4 + 4] = im * cos + re * sin
        for line in range(4):
            for c in range(2):
                high, low = halves(lines[c, pl.ds(line, 32, stride=4)])
                lines_hi[line * 32 : line * 32 + 32, c * 128 : c * 128 + 128] = high
                lines_lo[line * 32 : line * 32 + 32, c * 128 : c * 128 + 128] = low
        mixed = product(table, (lines_hi[...], lines_lo[...]), ((1,), (1,)))
        bands_out[part] = mixed.reshape(N_TILE, 2, 8, 128)
        send_part(tile_axis, part, *tile_refs)
        bands_in[part, tile_here] = bands_out[part, tile_here]

    for part in range(PARTS):
        wait_part(tile_axis, part, *tile_refs)
        points = fft_points([(bands_in[part, k, 0], bands_in[part, k, 1]) for k in range(N_TILE)], 1.0)
        for low, (re, im) in enumerate(points):
            cells[0, part, low], cells[1, part, low] = turn(re, im, 2.0 * math.pi * low * part / 64)

    @pl.loop(0, 4)
    def _(chunk):
        span = pl.ds(chunk * 4, 4)
        tables = [(turn_j[0, where], turn_j[1, where]) for where in (pl.ds(16 * g + chunk * 4, 4) for g in range(4))]
        points = fft_points([(cells[0, q, span], cells[1, q, span]) for q in range(4)], 1.0)
        points = [(re * c - im * s, im * c + re * s) for (re, im), (c, s) in zip(points, tables)]
        points = fft_points(trade(points, 2, 32), 1.0)
        points = [(re * c - im * s, im * c + re * s) for (re, im), (c, s) in zip(points, turn_h)]
        points = fft_points(trade(points, 1, 2), 1.0)
        excess = []
        for h, (re, im) in enumerate(points):
            start = pl.multiple_of((16 * h + chunk * 4) * 8, 32)
            rest = re * re + im * im - image[pl.ds(start, 32), :].reshape(4, 8, 128)
            excess.append((rest * re, rest * im))
        points = trade(fft_points(excess, -1.0), 1, 2)
        points = [(re * c + im * s, im * c - re * s) for (re, im), (c, s) in zip(points, turn_h)]
        points = trade(fft_points(points, -1.0), 2, 32)
        points = [(re * c + im * s, im * c - re * s) for (re, im), (c, s) in zip(points, tables)]
        for q, (re, im) in enumerate(fft_points(points, -1.0)):
            cells[0, q, span] = re
            cells[1, q, span] = im

    back_refs = (back_out, back_in, back_send, back_recv)
    for part in range(PARTS):
        points = [
            turn(cells[0, part, low], cells[1, part, low], -2.0 * math.pi * low * part / 64) for low in range(16)
        ]
        for k, (re, im) in enumerate(fft_points(points, -1.0)):
            back_out[part, k, 0] = re
            back_out[part, k, 1] = im
        send_part(tile_axis, part, *back_refs)
        back_in[part, tile_here] = back_out[part, tile_here]

    grad_refs = (grad_out, grad_hbm, grad_send, grad_recv)
    own = []
    for part in range(PARTS):
        wait_part(tile_axis, part, *back_refs)
        mixed = product(halves(back_in[part].reshape(256, 128)), table, ((0,), (0,)))
        lines[0] = mixed[:, 0:128]
        lines[1] = mixed[:, 128:256]
        points = []
        for low in range(N_LED):
            re, im = (lines[c, pl.ds(low, 4, stride=32)] for c in range(2))
            cos, sin = turn_u[0, low : low + 1], turn_u[1, low : low + 1]
            points.append((re * cos + im * sin, im * cos - re * sin))
        for origin, (re, im) in enumerate(fft_points(points, -1.0)):
            pr, pi = pupil[part, origin, 0:4], pupil[part, origin, 4:8]
            grad_out[part, origin, 0:4] = pr * re + pi * im
            grad_out[part, origin, 4:8] = pr * im - pi * re
        send_part(led_axis, part, *grad_refs)
        own.append(
            pltpu.make_async_copy(grad_out.at[part, led_here], grad_hbm.at[part, led_here], own_sem.at[part])
        )
        own[-1].start()

    wait_sent(led_axis, *led_refs)
    wait_sent(tile_axis, *tile_refs)
    wait_sent(tile_axis, *back_refs)
    for part in range(PARTS):
        own[part].wait()
        wait_part(led_axis, part, *grad_refs)
    wait_sent(led_axis, *grad_refs)


def update_kernel(
    led_any, row_any, col_any, spec_ref, grad_hbm, out_hbm, led_ref, row_ref, col_ref, rows_ref, work, grad_ref,
    load_sem, store_sem,
):
    led_here = lax.axis_index("led")
    tile_here = lax.axis_index("tile")
    loads = [
        pltpu.make_async_copy(src, dst, load_sem.at[k])
        for k, (src, dst) in enumerate(
            ((grad_hbm, grad_ref), (led_any, led_ref), (row_any, row_ref), (col_any, col_ref))
        )
    ]
    for load in loads:
        load.start()
    work[:, 0:16] = spec_ref[:, 0:16]
    for load in loads[1:]:
        load.wait()

    @pl.loop(0, N_LED, unroll=4)
    def _(slot):
        rows_ref[slot] = window_row(led_ref, row_ref, col_ref, slot, tile_here, led_here)

    loads[0].wait()
    low = lax.broadcasted_iota(jnp.int32, (8, 128), 0) < 4
    stores = []
    for c in range(2):
        if c == 1:
            work[:, 16:32] = spec_ref[:, 16:32]

        @pl.loop(0, N_LED, unroll=8)
        def _(slot):
            row = rows_ref[slot]
            for half in range(2):
                first, second = grad_ref[2 * half, slot], grad_ref[2 * half + 1, slot]
                if c == 0:
                    step = jnp.where(low, first, pltpu.roll(second, 4, 0))
                else:
                    step = jnp.where(low, pltpu.roll(first, 4, 0), second)
                span = slice(c * 16 + half * 8, c * 16 + half * 8 + 8)
                work[row, span] = work[row, span] - STEP_SIZE * step

        side = pl.ds(c * 16, 16)
        stores.append(pltpu.make_async_copy(work.at[:, side], out_hbm.at[:, side], store_sem.at[c]))
        stores[c].start()
    for store in stores:
        store.wait()


def shards(spectrum, intensities, led_of_slot, row_offset, col_offset, tile_mask, aberration):
    rows = spectrum.reshape(GR * GC, 2 * LINES, 128)
    masks = jnp.transpose(tile_mask, (1, 2, 0)).reshape(64, N_LED)
    hbm = pl.BlockSpec(memory_space=pltpu.HBM)
    vmem = pl.BlockSpec(memory_space=pltpu.VMEM)
    message = pltpu.VMEM((PARTS, N_LED, 8, 128), jnp.float32)
    band = pltpu.VMEM((PARTS, N_TILE, 2, 8, 128), jnp.float32)
    table = pltpu.VMEM((256, 256), jnp.bfloat16)
    lines = pltpu.VMEM((128, 256), jnp.bfloat16)
    sems = pltpu.SemaphoreType.DMA((PARTS,))
    grad = pl.pallas_call(
        exchange_kernel,
        out_shape=jax.ShapeDtypeStruct((PARTS, N_LED, 8, 128), jnp.float32),
        in_specs=[hbm] * 7,
        out_specs=hbm,
        scratch_shapes=[
            pltpu.SMEM((N_LED,), jnp.int32),
            pltpu.SMEM((N_LED,), jnp.int32),
            pltpu.SMEM((N_LED,), jnp.int32),
            pltpu.SMEM((64, N_LED), jnp.int32),
            pltpu.SMEM((5,), jnp.float32),
            pltpu.VMEM((GR * GC, 2 * LINES, 128), jnp.float32),
            pltpu.VMEM((1, BAND, M), jnp.bfloat16),
            pltpu.VMEM((512, 128), jnp.float32),
            table,
            table,
            pltpu.VMEM((2, 32, 128), jnp.float32),
            pltpu.VMEM((2, 64, 8, 128), jnp.float32),
            message,
            message,
            message,
            pltpu.VMEM((2, 128, 128), jnp.float32),
            lines,
            lines,
            band,
            band,
            pltpu.VMEM((2, PARTS, 16, 8, 128), jnp.float32),
            band,
            band,
            message,
            pltpu.SemaphoreType.DMA((7,)),
            pltpu.SemaphoreType.DMA((PARTS,)),
        ]
        + [sems] * 8,
        compiler_params=pltpu.CompilerParams(
            collective_id=0, has_side_effects=True, vmem_limit_bytes=56 * 1024 * 1024
        ),
    )(*(pltpu.with_memory_space_constraint(x, pltpu.HBM) for x in (led_of_slot, row_offset, col_offset, masks, aberration, rows, intensities)))
    updated = pl.pallas_call(
        update_kernel,
        out_shape=jax.ShapeDtypeStruct((GR * GC, 2 * LINES, 128), jnp.float32),
        in_specs=[pl.BlockSpec(memory_space=pl.ANY)] * 3 + [vmem, hbm],
        out_specs=hbm,
        scratch_shapes=[
            pltpu.SMEM((N_LED,), jnp.int32),
            pltpu.SMEM((N_LED,), jnp.int32),
            pltpu.SMEM((N_LED,), jnp.int32),
            pltpu.SMEM((N_LED,), jnp.int32),
            pltpu.VMEM((GR * GC, 2 * LINES, 128), jnp.float32),
            message,
            pltpu.SemaphoreType.DMA((4,)),
            pltpu.SemaphoreType.DMA((2,)),
        ],
        compiler_params=pltpu.CompilerParams(vmem_limit_bytes=8 * 1024 * 1024),
    )(led_of_slot, row_offset, col_offset, rows, pltpu.with_memory_space_constraint(grad, pltpu.HBM))
    return updated.reshape(spectrum.shape)


def solution(mesh):
    placed = (P(None, None, "tile", "led", None), P("led", "tile", None), P(), P(), P(), P(), P())
    return jax.shard_map(
        shards,
        mesh=mesh,
        in_specs=placed,
        out_specs=P(None, None, "tile", "led", None),
        check_vma=False,
    )
```
